256 devices in a mesh: lev: 4 (over x), wav: 64 (over z, y, core).
Axes of the slice: x: 4, y: 4, z: 8, core: 2. Of those that a mesh axis runs over, the one named last changes fastest.
Arguments:
- grid_field: bfloat16 [128, 640, 1280], P('lev', 'wav'), may hold values from -6 to 6
- legendre: bfloat16 [640, 640, 640], P('wav'), may hold values from -0.25 to 0.25
- wave_of_slot: int32 [640], replicated, may hold values from 0 to 639, each once
- lat_of_row: int32 [640], P('wav'), may hold values from 0 to 639, each once
- analysis: bfloat16 [128, 128], replicated, may hold values from -0.5 to 0.5
- synthesis: bfloat16 [128, 128], replicated, may hold values from -0.5 to 0.5
- mode_rates: float32 [128], replicated, may hold values from 0.05 to 5
- flux_weights: float32 [128], replicated, may hold values from -0.5 to 0.5
- remap_mats: bfloat16 [4, 4096, 128, 128], P('lev', 'wav'), may hold values from -0.5 to 0.5
- pair_dest: int32 [4, 4096, 1], P('lev'), may hold values from 0 to 63; in each aligned block of 64 rows (0 to 63, 64 to 127, ..., all dimensions but the last counted through in order) at most 2 rows name the same one
- pair_src: int32 [4, 4096], P('lev'), may hold values from 0 to 99
- pair_dst: int32 [4, 4096], P('lev'), may hold values from 0 to 47
- ocean_temp: float32 [8, 192, 8192], P(None, 'lev', 'wav'), may hold values from -6 to 6
- diffusivity: float32 [192, 8192], P('lev', 'wav'), may hold values from 0.05 to 0.24
- surface_heat: float32 [192, 8192], P('lev', 'wav'), may hold values from -4 to 4
- land_mask: int32 [192, 8192], P('lev', 'wav'), may hold values 0 or 1
Outputs:
- atm_out: bfloat16 [128, 640, 1280], P('lev', 'wav')
- ocean_out: float32 [8, 192, 8192], P(None, 'lev', 'wav')
- ocean_flux: float32 [192, 8192], P('lev', 'wav')
The draws below stay inside these ranges and needn't reach their ends.
Inputs may be any that keep to these rules, and one draw needn't show every extreme that they name: `wave_of_slot`: each wavenumber names exactly one slot. `lat_of_row`: each latitude names exactly one row. `pair_dest`: within the pairs of one source owner (aligned blocks of 64 pairs of a level row) no destination column is named more than 2 times.
All inputs are finite; a program needn't handle non-finite values. No bound on the sum of `land_mask` on one device may be relied on, other than what follows from the above.
Results may differ from the reference program's by a relative error of at most 0.015.
Values may be sent and summed in bfloat16 or wider, within the bound.
A program may use at most 128 MiB of HBM per device.

```python
import math
import jax
import jax.numpy as jnp
import numpy as np
from jax import lax

NLON = 1280
NLAT = 640
WAVES = 640
LEVELS = 128
OLEV = 8
OX = 48
OY = 128
CAP = 2
SWEEPS = 4
ASEG = 100
PAIRS_DEV = 64
PAIRS_ROW = 4096
O_ROWS = 192
O_COLS = 8192
N_LEV = 4
N_WAV = 64


def place_ends(values, rng, least, top_value):
    spot = [jax.random.randint(jax.random.fold_in(rng, axis), (), 0, length) for axis, length in enumerate(values.shape)]
    main_axis = values.shape.index(max(values.shape))
    beside = spot[:main_axis] + [(spot[main_axis] + 1) % values.shape[main_axis]] + spot[main_axis + 1:]
    return values.at[tuple(spot)].set(least).at[tuple(beside)].set(top_value)


def levels(own_key, dims, split, low, top_value):
    loudness = 1.0
    for position, parts in split:
        draws = jax.random.uniform(jax.random.fold_in(jax.random.fold_in(own_key, 6), position), (parts,), jnp.float32, low / len(split), top_value / len(split))
        loudness = loudness * jnp.repeat(jnp.exp(draws), dims[position] // parts).reshape((-1,) + (1,) * (len(dims) - 1 - position))
    return loudness


def assign_block(own_key, own, number, rows, number_of, top, bound, skew):
    order = jax.random.permutation(own_key, number_of)
    heavy_load, common = shares(number_of, rows * top, bound, skew, True), shares(number_of, rows * top, bound, skew, False)
    places = jnp.arange(number_of)

    def named(sizes, rotation):
        used = int((sizes > 0).sum())
        fixed = max(1, used // 4)
        shifted = fixed + (places - fixed + rotation * (used - fixed)) % max(1, number_of - fixed)
        return jnp.zeros((number_of,), jnp.int32).at[order[jnp.where(places < fixed, places, shifted)]].set(jnp.asarray(sizes, jnp.int32))

    sizes = jnp.where(number % 4 == 0, named(heavy_load, number // 4), named(common, number - number // 4 - 1))
    mixed = jax.random.permutation(jax.random.fold_in(own, 3), number_of)
    giver, sink = mixed[0:number_of // 2 * 2:2], mixed[1:number_of // 2 * 2:2]
    margin = jnp.minimum(sizes[giver] - 1, bound - sizes[sink]) // 2
    margin = jnp.where((giver == order[0]) | (sink == order[0]) | (sizes[sink] == 0), 0, jnp.maximum(margin, 0))
    shifted = jax.random.randint(jax.random.fold_in(own, 4), (number_of // 2,), 0, 1 << 20) % (margin + 1)
    sizes = sizes.at[giver].add(-shifted).at[sink].add(shifted)
    members = jnp.searchsorted(jnp.cumsum(sizes), jnp.arange(rows * top), side="right").astype(jnp.int32)
    table = members.reshape(top, rows).T
    table = table[jax.random.permutation(jax.random.fold_in(own, 1), rows)]
    rotation = jax.random.randint(jax.random.fold_in(own, 2), (rows, 1), 0, top)
    return jnp.take_along_axis(table, (jnp.arange(top)[None, :] + rotation) % top, axis=1)


def shares(amount, total, most, skew, full):
    weights = [(1 << 20) // math.isqrt(rank ** skew) + 1 for rank in range(1, amount + 1)]
    largest = most if full else min(most, max(-(-total // amount), total * weights[0] // sum(weights)))
    least = 1 if total - largest >= amount - 1 else 0
    holding, surplus = [largest] + [least] * (amount - 1), total - largest - least * (amount - 1)
    while surplus > 0:
        movable = [i for i in range(1, amount) if holding[i] < largest] or [i for i in range(1, amount) if holding[i] < most]
        mass, left = sum([weights[i] for i in movable]), surplus
        for i in movable:
            addition = min(most - holding[i], max(1, left * weights[i] // mass), surplus)
            holding[i] = holding[i] + addition
            surplus = surplus - addition
    return np.array(holding)


def centred(rng, shape, scale, bound, pieces=(), kind=jnp.bfloat16):
    level = levels(rng, shape, pieces, -0.22, 0.18) if pieces else 1.0
    drawn = jax.random.normal(rng, shape, jnp.float32) * scale * level
    return jnp.minimum(jnp.maximum(drawn, -bound), bound).astype(kind)


def setup_inputs(seed: int = 0) -> dict:
    splits = jax.random.split(jax.random.key(seed), 17)
    grid_field = centred(splits[0], (LEVELS, NLAT, NLON), 1.0, 6.0, ((0, 4), (1, 64)))
    legendre = centred(splits[1], (WAVES, NLAT, WAVES), NLAT ** -0.5, 0.25, ((0, 64),))
    wave_of_slot = jax.random.permutation(splits[2], WAVES).astype(jnp.int32)
    lat_of_row = jax.random.permutation(splits[3], NLAT).astype(jnp.int32)
    analysis = centred(splits[4], (LEVELS, LEVELS), LEVELS ** -0.5, 0.5)
    synthesis = centred(splits[5], (LEVELS, LEVELS), LEVELS ** -0.5, 0.5)
    mode_rates = jnp.clip(jnp.exp(jax.random.uniform(splits[6], (LEVELS,), jnp.float32, math.log(0.05), math.log(5.0))), 0.05, 5.0)
    flux_weights = centred(splits[7], (LEVELS,), LEVELS ** -0.5, 0.5, (), jnp.float32)
    remap_mats = centred(splits[8], (N_LEV, PAIRS_ROW, OY, OY), OY ** -0.5, 0.5, ((0, 4), (1, 64)))
    pair_dest_keys = jax.random.split(jax.random.fold_in(splits[9], 1), N_LEV * PAIRS_ROW // PAIRS_DEV)
    pair_dest_turns = jax.random.permutation(jax.random.fold_in(splits[9], 3), N_LEV * PAIRS_ROW // PAIRS_DEV)
    pair_dest = jax.vmap(lambda own, number: assign_block(jax.random.fold_in(splits[9], 2), own, number, PAIRS_DEV, N_WAV, 1, CAP, 2))(pair_dest_keys, pair_dest_turns).reshape((N_LEV, PAIRS_ROW, 1))
    pair_src = place_ends(jax.random.randint(splits[10], (N_LEV, PAIRS_ROW), 0, ASEG), jax.random.fold_in(splits[10], 1), 0, ASEG - 1).astype(jnp.int32)
    pair_dst = place_ends(jax.random.randint(splits[11], (N_LEV, PAIRS_ROW), 0, OX), jax.random.fold_in(splits[11], 1), 0, OX - 1).astype(jnp.int32)
    ocean_temp = centred(splits[12], (OLEV, O_ROWS, O_COLS), 1.0, 6.0, ((1, 4), (2, 64)), jnp.float32)
    diffusivity = jnp.clip(0.05 + 0.19 * jax.random.uniform(splits[13], (O_ROWS, O_COLS), jnp.float32) ** levels(splits[13], (O_ROWS, O_COLS), ((0, 4), (1, 64)), -0.2, 0.2), 0.05, 0.24)
    surface_heat = centred(splits[14], (O_ROWS, O_COLS), 0.5, 4.0, ((0, 4), (1, 64)), jnp.float32)
    land_mask = place_ends((jax.random.randint(splits[15], (O_ROWS, O_COLS), 0, 4) < 3).astype(jnp.int32), jax.random.fold_in(splits[15], 1), 0, 1)
    return dict(grid_field=grid_field, legendre=legendre, wave_of_slot=wave_of_slot, lat_of_row=lat_of_row, analysis=analysis, synthesis=synthesis, mode_rates=mode_rates, flux_weights=flux_weights, remap_mats=remap_mats, pair_dest=pair_dest, pair_src=pair_src, pair_dst=pair_dst, ocean_temp=ocean_temp, diffusivity=diffusivity, surface_heat=surface_heat, land_mask=land_mask)


def column_table(wave_ids, halves, lon_count):
    longitude = jnp.arange(lon_count, dtype=jnp.int32)
    phases = longitude[:, None] * wave_ids[None, :] % lon_count
    angles = phases.astype(jnp.float32) * (2.0 * math.pi / lon_count)
    factor = math.sqrt(2.0 / lon_count)
    matrix = jnp.where(halves[None, :] == 0, factor * jnp.cos(angles), -factor * jnp.sin(angles))
    return matrix.astype(jnp.bfloat16)

def reference(grid_field, legendre, wave_of_slot, lat_of_row, analysis, synthesis, mode_rates, flux_weights, remap_mats, pair_dest, pair_src, pair_dst, ocean_temp, diffusivity, surface_heat, land_mask):
    positions = jnp.arange(2 * WAVES, dtype=jnp.int32)
    wave_matrix = column_table(jnp.repeat(wave_of_slot, 2), positions % 2, NLON)
    fourier = jnp.dot(grid_field.reshape(LEVELS * NLAT, NLON), wave_matrix, preferred_element_type=jnp.float32).astype(jnp.bfloat16)
    fourier = fourier.reshape(LEVELS, NLAT, WAVES, 2)
    degree = jnp.arange(WAVES, dtype=jnp.int32)
    damp_base = (degree * (degree + 1)).astype(jnp.float32) / (WAVES * WAVES)
    damping = 1.0 / (1.0 + mode_rates[:, None] * damp_base[None, :])
    analysis_wide = analysis.astype(jnp.float32)
    synthesis_wide = synthesis.astype(jnp.float32)

    def per_slot(slot_id):
        columns = lax.dynamic_index_in_dim(fourier, slot_id, 2, keepdims=False).astype(jnp.float32)
        legendre_slot = lax.dynamic_index_in_dim(legendre, slot_id, 0, keepdims=False).astype(jnp.float32)
        spectra = jnp.einsum('xrk,rn->kxn', columns, legendre_slot)
        retained = degree >= wave_of_slot[slot_id]
        spectra = jnp.where(retained[None, None, :], spectra, 0.0).astype(jnp.bfloat16)
        modal_coef = jnp.einsum('ix,kxn->kin', analysis_wide, spectra.astype(jnp.float32))
        modal_coef = (modal_coef * damping[None]).astype(jnp.bfloat16)
        solved = jnp.einsum('xi,kin->kxn', synthesis_wide, modal_coef.astype(jnp.float32)).astype(jnp.bfloat16)
        solved_wide = solved.astype(jnp.float32)
        flux_coef = jnp.einsum('x,kxn->kn', flux_weights, solved_wide).astype(jnp.bfloat16)
        grid_coef = jnp.einsum('rn,kxn->kxr', legendre_slot, solved_wide).astype(jnp.bfloat16)
        flux_lat = jnp.einsum('rn,kn->kr', legendre_slot, flux_coef.astype(jnp.float32)).astype(jnp.bfloat16)
        return (grid_coef, flux_lat)
    grid_coef, flux_lat = lax.map(per_slot, jnp.arange(WAVES, dtype=jnp.int32))
    coef_flat = grid_coef.reshape(2 * WAVES, LEVELS * NLAT)
    regridded = lax.dot_general(coef_flat, wave_matrix, (((0,), (1,)), ((), ())), preferred_element_type=jnp.float32)
    flux_flat = flux_lat.reshape(2 * WAVES, NLAT)
    flux_grid = lax.dot_general(flux_flat, wave_matrix, (((0,), (1,)), ((), ())), preferred_element_type=jnp.float32).astype(jnp.bfloat16)
    latitude = jnp.sin(math.pi * (lat_of_row.astype(jnp.float32) + 0.5) / NLAT - math.pi / 2)
    atm_out = (regridded.reshape(LEVELS, NLAT, NLON) * (1.0 + grid_field.astype(jnp.float32) * latitude[None, :, None])).astype(jnp.bfloat16)
    ocean_mask = land_mask.astype(jnp.float32)
    level_one = (jnp.arange(OLEV, dtype=jnp.int32) == 0).astype(jnp.float32)[:, None, None]
    ocean_now = ocean_temp * ocean_mask[None]
    for sweep_idx in range(SWEEPS):
        padded = jnp.pad(ocean_now, ((0, 0), (1, 1), (1, 1)))
        laplace = padded[:, 2:, 1:-1] + padded[:, :-2, 1:-1] + padded[:, 1:-1, 2:] + padded[:, 1:-1, :-2] - 4.0 * ocean_now
        ocean_now = ocean_mask[None] * (ocean_now + diffusivity[None] * laplace + level_one * surface_heat[None])
    segments = flux_grid.reshape(NLAT * (NLON // OY), OY)
    source = jnp.arange(PAIRS_ROW, dtype=jnp.int32) // PAIRS_DEV

    def per_row(row_data):
        row_mats, row_dest, row_src, row_dst = row_data
        chosen = segments[source * ASEG + row_src].astype(jnp.float32)
        products = jnp.einsum('pij,pj->pi', row_mats.astype(jnp.float32), chosen)
        target = row_dst * N_WAV + row_dest[:, 0]
        return jax.ops.segment_sum(products, target, num_segments=OX * N_WAV)
    rows_out = lax.map(per_row, (remap_mats, pair_dest, pair_src, pair_dst))
    ocean_flux = rows_out.reshape(N_LEV * OX, N_WAV * OY)
    return (atm_out, ocean_now, ocean_flux)
```

```python
import functools
import math

import jax
import jax.numpy as jnp
from jax import lax
from jax.experimental import pallas as pl
from jax.experimental.pallas import tpu as pltpu
from jax.sharding import PartitionSpec as P

MESH = pl.DeviceIdType.MESH
F32 = jnp.float32
BF16 = jnp.bfloat16
HIGH = lax.Precision.HIGHEST

SWEEPS = 4
NG = 4
NW = 64
ND = NG * NW
LEV = 32
ROWS = 10
LON = 1280
WAVES = 640
NLEV = 128
COLS = 5
SLOTS = 3
MSG = 16
SENT = 14
PAIRS = 64
OX = 48
OLEV = 8
HALO = 8
EXT = OX + 2 * HALO
FIELDS = OLEV + 3

SIN_POLY = (6.28318528, -41.34168068, 81.60248108, -76.58128818, 39.76072297)


def nt(a, b):
    return lax.dot_general(a, b, (((1,), (1,)), ((), ())), preferred_element_type=F32)


def tn(a, b, precision=None):
    return lax.dot_general(
        a, b, (((0,), (0,)), ((), ())), preferred_element_type=F32, precision=precision
    )


def cos_turns(phase, scale):
    whole = jnp.floor(phase * (1.0 / LON) + 0.5)
    rest = jnp.abs(phase - whole * LON)
    t = (LON / 4 - rest) * (1.0 / LON)
    z = t * t
    c = [scale * v for v in SIN_POLY]
    return t * (c[0] + z * (c[1] + z * (c[2] + z * (c[3] + z * c[4]))))


def swap_blocks(v, lane):
    low = lane < 64
    even = lax.rem(lane // 32, 2) == 0
    a0 = jnp.where(low, v[0], pltpu.roll(v[2], 64, 1))
    a2 = jnp.where(low, pltpu.roll(v[0], 64, 1), v[2])
    a1 = jnp.where(low, v[1], pltpu.roll(v[3], 64, 1))
    a3 = jnp.where(low, pltpu.roll(v[1], 64, 1), v[3])
    return (
        jnp.where(even, a0, pltpu.roll(a1, 32, 1)),
        jnp.where(even, pltpu.roll(a0, 96, 1), a1),
        jnp.where(even, a2, pltpu.roll(a3, 32, 1)),
        jnp.where(even, pltpu.roll(a2, 96, 1), a3),
    )


def lanes(shape):
    return lax.broadcasted_iota(jnp.int32, shape, len(shape) - 1)


def down(row):
    return jnp.broadcast_to(row, (128, 128)).T


def kernel(
    wos_s,
    lat_s,
    field,
    legendre,
    wos_t,
    analysis,
    synthesis,
    rates,
    weights,
    mats,
    pairs,
    temp,
    kappa,
    heat,
    mask,
    atm,
    ocean,
    flux,
    table,
    rows_in,
    wide,
    acc,
    out1,
    in1,
    in2,
    leg,
    cols_f,
    flux_f,
    lhs,
    segs,
    mats_v,
    out3,
    in3,
    edge,
    rows_edge,
    in_rows,
    slab,
    in_slab,
    ext,
    local_sem,
    send1,
    recv1,
    send2,
    recv2,
    send3,
    recv3,
    send4,
    recv4,
):
    g = lax.axis_index("lev")
    w = lax.axis_index("wav")
    me = g * NW + w
    barrier = pltpu.get_barrier_semaphore()

    first_slot = (COLS * g) // 2
    leg_copy = pltpu.make_async_copy(
        legendre.at[pl.ds(first_slot, SLOTS)], leg, local_sem.at[0]
    )
    leg_copy.start()
    mats_copy = pltpu.make_async_copy(mats.at[0], mats_v, local_sem.at[1])
    mats_copy.start()

    def greet(j, c):
        there = lax.rem(w + j, NW)
        for i in range(NG):
            pl.semaphore_signal(
                barrier, inc=1, device_id=(lax.rem(g + i, NG), there), device_id_type=MESH
            )
        return c

    lax.fori_loop(1, NW, greet, 0)
    for i in range(1, NG):
        pl.semaphore_signal(
            barrier, inc=1, device_id=(lax.rem(g + i, NG), w), device_id_type=MESH
        )

    def spread(x, c):
        v = field[x]
        for jt in range(10):
            wide[jt, pl.ds(pl.multiple_of(x * 16, 16), ROWS), :] = v[
                :, jt * 128 : (jt + 1) * 128
            ].astype(F32)
        return c

    lax.fori_loop(0, LEV, spread, 0)
    for r in range(ROWS):
        for jt in range(10):
            rows_in[r * LEV : (r + 1) * LEV, jt * 128 : (jt + 1) * 128] = wide[
                jt, pl.ds(r, LEV, stride=16), :
            ].astype(BF16)
    rows_in[320:384, :] = rows_in[256:320, :]

    ocean_mask = mask[...].astype(F32)
    for k in range(OLEV):
        edge[k] = temp[k] * ocean_mask
    edge[OLEV] = ocean_mask
    edge[OLEV + 1] = kappa[...]
    edge[OLEV + 2] = heat[...]
    lane48 = lanes((OX, 128))
    left = jnp.zeros((OX, 128), F32)
    right = jnp.zeros((OX, 128), F32)
    for k in range(FIELDS):
        here = lane48 // 4 == k
        v = edge[k]
        left = jnp.where(here, pltpu.roll(v, 4 * k, 1) if k else v, left)
        right = jnp.where(here, pltpu.roll(v, (4 * k + 4) % 128, 1), right)
        rows_edge[0, k] = v[:HALO]
        rows_edge[1, k] = v[OX - HALO :]
    slab[0] = left
    slab[1] = right

    up, dn = lax.rem(g + NG - 1, NG), lax.rem(g + 1, NG)
    wl, wr = lax.rem(w + NW - 1, NW), lax.rem(w + 1, NW)

    def ocean_copies():
        c = []
        c.append((rows_edge.at[0], in_rows.at[1], (up, w)))
        c.append((rows_edge.at[1], in_rows.at[0], (dn, w)))
        for side, ww in ((0, wl), (1, wr)):
            c.append((slab.at[side], in_slab.at[1 - side, pl.ds(HALO, OX)], (g, ww)))
            c.append(
                (slab.at[side, pl.ds(0, HALO)], in_slab.at[1 - side, pl.ds(HALO + OX, HALO)], (up, ww))
            )
            c.append(
                (slab.at[side, pl.ds(OX - HALO, HALO)], in_slab.at[1 - side, pl.ds(0, HALO)], (dn, ww))
            )
        return [
            pltpu.make_async_remote_copy(
                src_ref=s, dst_ref=d, send_sem=send4.at[i], recv_sem=recv4.at[i],
                device_id=dev, device_id_type=MESH,
            )
            for i, (s, d, dev) in enumerate(c)
        ]

    lane64 = lanes((NW, 128))

    def make_group(i, c):
        gg = lax.rem(g + i, NG)
        base = pl.multiple_of(gg * (COLS * NW), NW)
        for cl in range(COLS):
            q = gg * COLS + cl
            row = wos_t[pl.ds(q // 2, 1), :]
            m = down(row.astype(F32))[:NW]
            shift = (lax.rem(q, 2) * (LON // 4)).astype(F32)
            scale = math.sqrt(2.0 / LON)
            phase = m * lane64.astype(F32) + shift
            now = cos_turns(phase, scale)
            before = cos_turns(phase - 128.0 * m, scale)
            twice = cos_turns(128.0 * m, 2.0)
            for a in range(10):
                table[pl.ds(base + cl * NW, NW), a * 128 : (a + 1) * 128] = now.astype(BF16)
                now, before = twice * now - before, now
        out = nt(table[pl.ds(base, COLS * NW), :], rows_in[...])
        start = pl.multiple_of(gg * (NW * MSG), NW * MSG)
        prev = None
        for cl in range(COLS):
            o = out[cl * NW : (cl + 1) * NW]
            acc[pl.ds(start + 2 * cl, NW, stride=MSG), :] = o[:, :128]
            acc[pl.ds(start + 2 * cl + 1, NW, stride=MSG), :] = o[:, 128:256]
            if cl % 2 == 0:
                prev = o[:, 256:384]
            if cl % 2 == 1 or cl == COLS - 1:
                acc[pl.ds(start + 10 + cl // 2, NW, stride=MSG), :] = jnp.where(
                    lane64 < 64, prev, o[:, 256:384]
                )
        out1[pl.ds(gg * NW, NW)] = (
            acc[pl.ds(start, NW * MSG), :].reshape(NW, MSG, 128).astype(BF16)
        )

        @pl.when(i == 0)
        def _():
            pl.semaphore_wait(barrier, ND - 1)
            for copy in ocean_copies():
                copy.start()
            in1[me] = out1[me]

        def send(j, c):
            there = lax.rem(w + j, NW)
            pltpu.make_async_remote_copy(
                src_ref=out1.at[gg * NW + there, pl.ds(0, SENT)],
                dst_ref=in1.at[me, pl.ds(0, SENT)],
                send_sem=send1,
                recv_sem=recv1,
                device_id=(gg, there),
                device_id_type=MESH,
            ).start()
            return c

        lax.fori_loop(jnp.where(i == 0, 1, 0), NW, send, 0)
        return c

    lax.fori_loop(0, NG, make_group, 0)

    for copy in ocean_copies():
        copy.wait()
    sub_e = lax.broadcasted_iota(jnp.int32, (EXT, 256), 0)
    lane_e = lanes((EXT, 256))
    inside_rows = jnp.logical_and(
        jnp.logical_or(sub_e >= HALO, g > 0),
        jnp.logical_or(sub_e < HALO + OX, g < NG - 1),
    )
    inside = jnp.logical_and(
        inside_rows,
        jnp.logical_and(
            jnp.logical_or(lane_e < 252, w > 0),
            jnp.logical_or(jnp.logical_or(lane_e < 128, lane_e >= 252), w < NW - 1),
        ),
    )
    lane_m = lanes((EXT, 128))
    for k in range(FIELDS):
        ext[k, :HALO, :128] = in_rows[0, k]
        ext[k, HALO : HALO + OX, :128] = edge[k]
        ext[k, HALO + OX :, :128] = in_rows[1, k]
        from_left = pltpu.roll(in_slab[0], (124 - 4 * k) % 128, 1)
        from_right = pltpu.roll(in_slab[1], (128 - 4 * k) % 128, 1) if k else in_slab[1]
        ext[k, :, 128:] = jnp.where(
            lane_m >= 124, from_left, jnp.where(lane_m < 4, from_right, 0.0)
        )
    e_mask = jnp.where(inside, ext[OLEV], 0.0)
    ext[OLEV] = e_mask
    for k in range(2):
        ext[OLEV + 1 + k] = jnp.where(inside, ext[OLEV + 1 + k], 0.0)

    def level(k, c):
        cur = jnp.where(inside, ext[k], 0.0)
        add = jnp.where(k == 0, 1.0, 0.0).astype(F32) * ext[OLEV + 2]
        for _ in range(SWEEPS):
            lap = (
                pltpu.roll(cur, EXT - 1, 0)
                + pltpu.roll(cur, 1, 0)
                + pltpu.roll(cur, 255, 1)
                + pltpu.roll(cur, 1, 1)
                - 4.0 * cur
            )
            cur = ext[OLEV] * (cur + ext[OLEV + 1] * lap + add)
        ocean[k] = cur[HALO : HALO + OX, :128]
        return c

    lax.fori_loop(0, OLEV, level, 0)

    sub_p = lax.broadcasted_iota(jnp.int32, (PAIRS, PAIRS), 0)
    lane_p = lanes((PAIRS, PAIRS))
    upper = (sub_p < lane_p).astype(BF16)
    dest_all = pairs[0]
    hits = dest_all == w
    rank_in = jnp.dot(hits.astype(BF16), upper, preferred_element_type=F32)
    lane_o = lanes((PAIRS, 128))
    pick_in = []
    for s in range(2):
        chosen_s = jnp.logical_and(hits, rank_in == float(s))
        row_of = jnp.sum(
            jnp.where(chosen_s, pairs[2].astype(F32) + 1.0, 0.0), axis=1, keepdims=True
        )
        pick_in.append((lane_o.astype(F32) + 1.0 == row_of).astype(F32))
    my_dest = pairs[0, pl.ds(w, 1), :]
    my_src = pairs[1, pl.ds(w, 1), :]
    same = sub_p == my_dest
    counts = jnp.dot(same.astype(BF16), upper, preferred_element_type=F32)
    rank_out = jnp.sum(jnp.where(same, counts, 0.0), axis=0, keepdims=True)
    pick_out = [
        jnp.logical_and(same, rank_out == float(s)).astype(F32) for s in range(2)
    ]
    src_row = my_src // 10
    seg_at = (my_src - src_row * 10) * 16 + src_row
    pick_seg = (lax.broadcasted_iota(jnp.int32, (160, PAIRS), 0) == seg_at).astype(BF16)

    degree = lanes((NLEV, WAVES))
    base = (degree * (degree + 1)).astype(F32) / float(WAVES * WAVES)
    rate = down(rates[...])
    weight = down(weights[...])
    damping = 1.0 / (1.0 + jnp.concatenate([rate] * 5, axis=1) * base)
    leg_copy.wait()

    def all_but_one(send_sem, recv_sem, src, dst):
        return pltpu.make_async_remote_copy(
            src_ref=src.at[pl.ds(0, ND - 1), pl.ds(0, SENT)],
            dst_ref=dst.at[pl.ds(0, ND - 1), pl.ds(0, SENT)],
            send_sem=send_sem,
            recv_sem=recv_sem,
            device_id=(g, w),
            device_id_type=MESH,
        )

    def widen(src):
        def step(i, c):
            n = ND // 16
            acc[pl.ds(pl.multiple_of(i * n * MSG, n * MSG), n * MSG), :] = (
                src[pl.ds(i * n, n)].astype(F32).reshape(n * MSG, 128)
            )
            return c

        lax.fori_loop(0, 16, step, 0)

    first = all_but_one(send1, recv1, out1, in1)
    first.wait_send()
    first.wait_recv()
    widen(in1)

    def at(ref, start, n, stride):
        return ref[pl.ds(start, n, stride=stride), :]

    for cl in range(COLS):
        for t in range(2):
            v = [at(acc, k * NW * MSG + 2 * cl + t, NW, MSG) for k in range(NG)]
            for q, out in enumerate(swap_blocks(v, lane64)):
                cols_f[pl.ds(cl * WAVES + 4 * t + q, NW, stride=ROWS), :] = out
    for p in range(3):
        v = [at(acc, k * NW * MSG + 10 + p, NW, MSG) for k in range(NG)]
        for q, out in enumerate(swap_blocks(v, lane64)):
            if 2 * p + q // 2 < COLS:
                cols_f[pl.ds((2 * p + q // 2) * WAVES + 8 + q % 2, NW, stride=ROWS), :] = out

    odd = lax.rem(g, 2)

    def column(cl, c):
        here = pl.ds(pl.multiple_of(cl * WAVES, WAVES), WAVES)
        table_of = leg[(odd + cl) // 2]
        m = wos_s[w * 10 + (COLS * g + cl) // 2]
        spectra = jnp.dot(
            cols_f[here, :].T.astype(BF16), table_of, preferred_element_type=F32
        )
        spectra = jnp.where(degree >= m, spectra, 0.0).astype(BF16)
        modal = jnp.dot(analysis[...], spectra, preferred_element_type=F32)
        modal = (modal * damping).astype(BF16)
        solved = jnp.dot(synthesis[...], modal, preferred_element_type=F32).astype(BF16)
        flux_coef = jnp.concatenate(
            [
                jnp.sum(
                    weight * solved[:, b * 128 : (b + 1) * 128].astype(F32),
                    axis=0,
                    keepdims=True,
                )
                for b in range(5)
            ],
            axis=1,
        )
        right = jnp.concatenate(
            [solved, jnp.broadcast_to(flux_coef, (128, WAVES)).astype(BF16)], axis=0
        )
        back = nt(table_of, right)
        cols_f[here, :] = back[:, :128]
        flux_f[here, :] = back[:, 128:]
        return c

    lax.fori_loop(0, COLS, column, 0)

    for cl in range(COLS):
        for t in range(2):
            v = [at(cols_f, cl * WAVES + 4 * t + q, NW, ROWS) for q in range(NG)]
            for k, out in enumerate(swap_blocks(v, lane64)):
                acc[pl.ds(k * NW * MSG + 2 * cl + t, NW, stride=MSG), :] = out
    fluxes = jnp.zeros((NW, 128), F32)
    for cl in range(COLS):
        for r in range(ROWS):
            fluxes = jnp.where(
                lane64 == 64 + cl * ROWS + r, at(flux_f, cl * WAVES + r, NW, ROWS), fluxes
            )
    for p in range(3):
        v = []
        for q in range(4):
            cl = min(2 * p + q // 2, COLS - 1)
            v.append(at(cols_f, cl * WAVES + 8 + q % 2, NW, ROWS))
        for k, out in enumerate(swap_blocks(v, lane64)):
            if p == 2:
                out = jnp.where(lane64 < 64, out, fluxes)
            acc[pl.ds(k * NW * MSG + 10 + p, NW, stride=MSG), :] = out

    def send_group(i, c):
        gg = lax.rem(g + i, NG)
        start = pl.multiple_of(gg * (NW * MSG), NW * MSG)
        out1[pl.ds(gg * NW, NW)] = (
            acc[pl.ds(start, NW * MSG), :].reshape(NW, MSG, 128).astype(BF16)
        )

        @pl.when(i == 0)
        def _():
            in2[me] = out1[me]

        def send(j, c):
            there = lax.rem(w + j, NW)
            pltpu.make_async_remote_copy(
                src_ref=out1.at[gg * NW + there, pl.ds(0, SENT)],
                dst_ref=in2.at[me, pl.ds(0, SENT)],
                send_sem=send2,
                recv_sem=recv2,
                device_id=(gg, there),
                device_id_type=MESH,
            ).start()
            return c

        lax.fori_loop(jnp.where(i == 0, 1, 0), NW, send, 0)
        return c

    lax.fori_loop(0, NG, send_group, 0)
    mats_copy.wait()
    second = all_but_one(send2, recv2, out1, in2)
    second.wait_send()
    second.wait_recv()
    widen(in2)

    for k in range(NG):
        f12 = at(acc, k * NW * MSG + 12, NW, MSG)
        for cl in range(COLS):
            rows = pl.ds((k * COLS + cl) * NW, NW)
            for t in range(2):
                lhs[rows, t * 128 : (t + 1) * 128] = at(
                    acc, k * NW * MSG + 2 * cl + t, NW, MSG
                ).astype(BF16)
            v = at(acc, k * NW * MSG + 10 + cl // 2, NW, MSG) if cl < 4 else f12
            if cl % 2 == 1:
                v = pltpu.roll(v, 64, 1)
            f = pltpu.roll(f12, 128 - cl * ROWS, 1) if cl else f12
            lhs[rows, 256:384] = jnp.where(
                lane64 < 64, v, jnp.where(lane64 < 64 + ROWS, f, 0.0)
            ).astype(BF16)
    last = tn(lhs[:, 256:384], table[...])
    for r in range(2):
        for jt in range(10):
            wide[jt, pl.ds(8 + r, LEV, stride=16), :] = last[
                r * LEV : (r + 1) * LEV, jt * 128 : (jt + 1) * 128
            ]
    for jt in range(10):
        segs[jt * 16 : (jt + 1) * 16, :] = last[64:80, jt * 128 : (jt + 1) * 128].astype(BF16)
    chosen = tn(pick_seg, segs[...]).astype(BF16)
    sub8 = lax.broadcasted_iota(jnp.int32, (8, 128), 0)
    parts = []
    for b in range(PAIRS // 8):
        total = jnp.zeros((8, 128), F32)
        eight = chosen[b * 8 : (b + 1) * 8]
        for u in range(8):
            total = jnp.where(sub8 == u, nt(eight, mats_v[b * 8 + u]), total)
        parts.append(total)
    products = jnp.concatenate(parts, axis=0)
    for s in range(2):
        out3[pl.ds(s, NW, stride=8), :] = jnp.dot(
            pick_out[s], products, precision=HIGH, preferred_element_type=F32
        )
    in3[pl.ds(pl.multiple_of(w * 8, 8), 8), :] = out3[pl.ds(pl.multiple_of(w * 8, 8), 8), :]

    def send_flux(j, c):
        there = lax.rem(w + j, NW)
        pltpu.make_async_remote_copy(
            src_ref=out3.at[pl.ds(pl.multiple_of(there * 8, 8), 8)],
            dst_ref=in3.at[pl.ds(pl.multiple_of(w * 8, 8), 8)],
            send_sem=send3,
            recv_sem=recv3,
            device_id=(g, there),
            device_id_type=MESH,
        ).start()
        return c

    lax.fori_loop(1, NW, send_flux, 0)

    for t in range(2):
        main = tn(lhs[:, t * 128 : (t + 1) * 128], table[...])
        for q in range(4):
            for jt in range(10):
                wide[jt, pl.ds(4 * t + q, LEV, stride=16), :] = main[
                    q * LEV : (q + 1) * LEV, jt * 128 : (jt + 1) * 128
                ]
    sub16 = lax.broadcasted_iota(jnp.int32, (16, 128), 0)
    mu = jnp.zeros((16, 128), F32)
    for r in range(ROWS):
        mu = jnp.where(sub16 == r, lat_s[r].astype(F32), mu)
    mu = -cos_turns(mu + 0.5, 1.0)
    mu = mu[:ROWS]

    def finish(x, c):
        v = field[x].astype(F32)
        for jt in range(10):
            cut = slice(jt * 128, (jt + 1) * 128)
            grid = wide[jt, pl.ds(pl.multiple_of(x * 16, 16), ROWS), :]
            atm[x, :, cut] = (grid * (1.0 + v[:, cut] * mu)).astype(BF16)
        return c

    lax.fori_loop(0, LEV, finish, 0)

    third = pltpu.make_async_remote_copy(
        src_ref=out3.at[pl.ds(0, (NW - 1) * 8)],
        dst_ref=in3.at[pl.ds(0, (NW - 1) * 8)],
        send_sem=send3,
        recv_sem=recv3,
        device_id=(g, w),
        device_id_type=MESH,
    )
    third.wait_send()
    third.wait_recv()
    summed = jnp.zeros((128, 128), F32)
    for s in range(2):
        summed = summed + tn(pick_in[s], at(in3, s, NW, 8), HIGH)
    flux[...] = summed[:OX]


def per_device(
    grid_field,
    legendre,
    wave_of_slot,
    lat_of_row,
    analysis,
    synthesis,
    mode_rates,
    flux_weights,
    remap_mats,
    pair_dest,
    pair_src,
    pair_dst,
    ocean_temp,
    diffusivity,
    surface_heat,
    land_mask,
):
    waves = jnp.pad(wave_of_slot.reshape(NW, 10).T, ((0, 6), (0, 64)))
    pairs = jnp.stack([pair_dest.reshape(-1), pair_src.reshape(-1), pair_dst.reshape(-1)])
    pairs = pairs.reshape(3, NW, PAIRS)
    smem = pl.BlockSpec(memory_space=pltpu.SMEM)
    vmem = pl.BlockSpec(memory_space=pltpu.VMEM)
    anys = pl.BlockSpec(memory_space=pl.ANY)
    return pl.pallas_call(
        kernel,
        out_shape=(
            jax.ShapeDtypeStruct((LEV, ROWS, LON), BF16),
            jax.ShapeDtypeStruct((OLEV, OX, 128), F32),
            jax.ShapeDtypeStruct((OX, 128), F32),
        ),
        in_specs=[smem, smem, vmem, anys, vmem, vmem, vmem, vmem, vmem, anys]
        + [vmem] * 5,
        out_specs=(vmem, vmem, vmem),
        scratch_shapes=[
            pltpu.VMEM((LON, LON), BF16),
            pltpu.VMEM((384, LON), BF16),
            pltpu.VMEM((10, LEV * 16, 128), F32),
            pltpu.VMEM((ND * MSG, 128), F32),
            pltpu.VMEM((ND, MSG, 128), BF16),
            pltpu.VMEM((ND, MSG, 128), BF16),
            pltpu.VMEM((ND, MSG, 128), BF16),
            pltpu.VMEM((SLOTS, WAVES, WAVES), BF16),
            pltpu.VMEM((COLS * WAVES, 128), F32),
            pltpu.VMEM((COLS * WAVES, 128), F32),
            pltpu.VMEM((LON, 384), BF16),
            pltpu.VMEM((160, 128), BF16),
            pltpu.VMEM((PAIRS, 128, 128), BF16),
            pltpu.VMEM((NW * 8, 128), F32),
            pltpu.VMEM((NW * 8, 128), F32),
            pltpu.VMEM((FIELDS, OX, 128), F32),
            pltpu.VMEM((2, FIELDS, HALO, 128), F32),
            pltpu.VMEM((2, FIELDS, HALO, 128), F32),
            pltpu.VMEM((2, OX, 128), F32),
            pltpu.VMEM((2, EXT, 128), F32),
            pltpu.VMEM((FIELDS, EXT, 256), F32),
            pltpu.SemaphoreType.DMA((2,)),
            pltpu.SemaphoreType.DMA(()),
            pltpu.SemaphoreType.DMA(()),
            pltpu.SemaphoreType.DMA(()),
            pltpu.SemaphoreType.DMA(()),
            pltpu.SemaphoreType.DMA(()),
            pltpu.SemaphoreType.DMA(()),
            pltpu.SemaphoreType.DMA((8,)),
            pltpu.SemaphoreType.DMA((8,)),
        ],
        compiler_params=pltpu.CompilerParams(
            collective_id=0, has_side_effects=True, vmem_limit_bytes=60 * 1024 * 1024
        ),
        name="step",
    )(
        wave_of_slot,
        lat_of_row,
        grid_field,
        legendre,
        waves,
        analysis,
        synthesis,
        mode_rates.reshape(1, NLEV),
        flux_weights.reshape(1, NLEV),
        remap_mats,
        pairs,
        ocean_temp,
        diffusivity,
        surface_heat,
        land_mask,
    )


def solution(mesh):
    return jax.shard_map(
        per_device,
        mesh=mesh,
        in_specs=(
            P("lev", "wav", None),
            P("wav", None, None),
            P(),
            P("wav"),
            P(),
            P(),
            P(),
            P(),
            P("lev", "wav", None, None),
            P("lev", None, None),
            P("lev", None),
            P("lev", None),
            P(None, "lev", "wav"),
            P("lev", "wav"),
            P("lev", "wav"),
            P("lev", "wav"),
        ),
        out_specs=(P("lev", "wav", None), P(None, "lev", "wav"), P("lev", "wav")),
        check_vma=False,
    )
```

```python
import functools
import math

import jax
import jax.numpy as jnp
from jax import lax
from jax.experimental import pallas as pl
from jax.experimental.pallas import tpu as pltpu
from jax.sharding import PartitionSpec as P

MESH = pl.DeviceIdType.MESH
F32 = jnp.float32
BF16 = jnp.bfloat16
HIGH = lax.Precision.HIGHEST

SWEEPS = 4
NG = 4
NW = 64
ND = NG * NW
LEV = 32
ROWS = 10
LON = 1280
WAVES = 640
NLEV = 128
COLS = 5
SLOTS = 3
MSG = 16
SENT = 14
PAIRS = 64
OX = 48
OLEV = 8
HALO = 8
EXT = OX + 2 * HALO
FIELDS = OLEV + 3

SIN_POLY = (6.28318528, -41.34168068, 81.60248108, -76.58128818, 39.76072297)


def nt(a, b):
    return lax.dot_general(a, b, (((1,), (1,)), ((), ())), preferred_element_type=F32)


def tn(a, b, precision=None):
    return lax.dot_general(
        a, b, (((0,), (0,)), ((), ())), preferred_element_type=F32, precision=precision
    )


def cos_turns(phase, scale):
    whole = jnp.floor(phase * (1.0 / LON) + 0.5)
    rest = jnp.abs(phase - whole * LON)
    t = (LON / 4 - rest) * (1.0 / LON)
    z = t * t
    c = [scale * v for v in SIN_POLY]
    return t * (c[0] + z * (c[1] + z * (c[2] + z * (c[3] + z * c[4]))))


def swap_blocks(v, lane):
    low = lane < 64
    even = lax.rem(lane // 32, 2) == 0
    a0 = jnp.where(low, v[0], pltpu.roll(v[2], 64, 1))
    a2 = jnp.where(low, pltpu.roll(v[0], 64, 1), v[2])
    a1 = jnp.where(low, v[1], pltpu.roll(v[3], 64, 1))
    a3 = jnp.where(low, pltpu.roll(v[1], 64, 1), v[3])
    return (
        jnp.where(even, a0, pltpu.roll(a1, 32, 1)),
        jnp.where(even, pltpu.roll(a0, 96, 1), a1),
        jnp.where(even, a2, pltpu.roll(a3, 32, 1)),
        jnp.where(even, pltpu.roll(a2, 96, 1), a3),
    )


def lanes(shape):
    return lax.broadcasted_iota(jnp.int32, shape, len(shape) - 1)


def down(row):
    return jnp.broadcast_to(row, (128, 128)).T


def kernel(
    wos_s,
    lat_s,
    field,
    legendre,
    wos_v,
    analysis,
    synthesis,
    rates,
    weights,
    mats,
    p_dest,
    p_src,
    p_dst,
    temp,
    kappa,
    heat,
    mask,
    atm,
    ocean,
    flux,
    table,
    rows_in,
    waves,
    acc,
    out1,
    in1,
    in2,
    leg,
    cols_f,
    flux_f,
    lhs,
    segs,
    mats_v,
    out3,
    in3,
    edge,
    rows_edge,
    in_rows,
    slab,
    in_slab,
    ext,
    ready,
    local_sem,
    send1,
    recv1,
    send2,
    recv2,
    send3,
    recv3,
    send4,
    recv4,
):
    g = lax.axis_index("lev")
    w = lax.axis_index("wav")
    me = g * NW + w
    barrier = pltpu.get_barrier_semaphore()

    first_slot = (COLS * g) // 2
    leg_copy = pltpu.make_async_copy(
        legendre.at[pl.ds(first_slot, SLOTS)], leg, local_sem.at[0]
    )
    leg_copy.start()
    mats_copy = pltpu.make_async_copy(mats.at[0], mats_v, local_sem.at[1])
    mats_copy.start()

    low = lax.rem(w, 4)
    high = w // 4
    for i in range(NG):
        for j in range(4):
            if i or j:
                pl.semaphore_signal(
                    barrier,
                    inc=1,
                    device_id=(lax.rem(g + i, NG), high * 4 + lax.rem(low + j, 4)),
                    device_id_type=MESH,
                )
    for j in range(1, 16):
        pl.semaphore_signal(
            barrier,
            inc=1,
            device_id=(g, lax.rem(high + j, 16) * 4 + low),
            device_id_type=MESH,
        )

    for r in range(ROWS):
        rows_in[r * LEV : (r + 1) * LEV, :] = field[r]
    rows_in[320:352, :] = field[8]
    rows_in[352:384, :] = field[9]

    sub_w = lax.broadcasted_iota(jnp.int32, (NW, WAVES), 0)
    at_slot = lanes((NW, WAVES)) - 10 * sub_w
    all_waves = jnp.broadcast_to(wos_v[...].reshape(1, WAVES).astype(F32), (NW, WAVES))
    for k in range(10):
        m = jnp.sum(jnp.where(at_slot == k, all_waves, 0.0), axis=1, keepdims=True)
        waves[k] = jnp.broadcast_to(m, (NW, 128))

    ocean_mask = mask[...].astype(F32)
    for k in range(OLEV):
        edge[k] = temp[k] * ocean_mask
    edge[OLEV] = ocean_mask
    edge[OLEV + 1] = kappa[...]
    edge[OLEV + 2] = heat[...]
    lane48 = lanes((OX, 128))
    left = jnp.zeros((OX, 128), F32)
    right = jnp.zeros((OX, 128), F32)
    for k in range(FIELDS):
        here = lane48 // 4 == k
        v = edge[k]
        left = jnp.where(here, pltpu.roll(v, 4 * k, 1) if k else v, left)
        right = jnp.where(here, pltpu.roll(v, (4 * k + 4) % 128, 1), right)
        rows_edge[0, k] = v[:HALO]
        rows_edge[1, k] = v[OX - HALO :]
    slab[0] = left
    slab[1] = right

    up, dn = lax.rem(g + NG - 1, NG), lax.rem(g + 1, NG)
    wl, wr = lax.rem(w + NW - 1, NW), lax.rem(w + 1, NW)

    def ocean_copies():
        c = []
        c.append((rows_edge.at[0], in_rows.at[1], (up, w)))
        c.append((rows_edge.at[1], in_rows.at[0], (dn, w)))
        for side, ww in ((0, wl), (1, wr)):
            c.append((slab.at[side], in_slab.at[1 - side, pl.ds(HALO, OX)], (g, ww)))
            c.append(
                (slab.at[side, pl.ds(0, HALO)], in_slab.at[1 - side, pl.ds(HALO + OX, HALO)], (up, ww))
            )
            c.append(
                (slab.at[side, pl.ds(OX - HALO, HALO)], in_slab.at[1 - side, pl.ds(0, HALO)], (dn, ww))
            )
        return [
            pltpu.make_async_remote_copy(
                src_ref=s, dst_ref=d, send_sem=send4.at[i], recv_sem=recv4.at[i],
                device_id=dev, device_id_type=MESH,
            )
            for i, (s, d, dev) in enumerate(c)
        ]

    lane64 = lanes((NW, 128))

    def make_group(i, c):
        gg = lax.rem(g + i, NG)
        base = pl.multiple_of(gg * (COLS * NW), NW)
        for cl in range(COLS):
            q = gg * COLS + cl
            m = waves[q // 2]
            shift = (lax.rem(q, 2) * (LON // 4)).astype(F32)
            scale = math.sqrt(2.0 / LON)
            phase = m * lane64.astype(F32) + shift
            now = cos_turns(phase, scale)
            before = cos_turns(phase - 128.0 * m, scale)
            twice = cos_turns(128.0 * m, 2.0)
            for a in range(10):
                table[pl.ds(base + cl * NW, NW), a * 128 : (a + 1) * 128] = now.astype(BF16)
                now, before = twice * now - before, now
        @pl.when(i == 0)
        def _():
            pl.semaphore_wait(barrier, 30)
            for j in range(1, 16):
                pl.semaphore_signal(
                    ready,
                    inc=1,
                    device_id=(g, lax.rem(high + j, 16) * 4 + low),
                    device_id_type=MESH,
                )

        out = nt(table[pl.ds(base, COLS * NW), :], rows_in[...])
        start = pl.multiple_of(gg * (NW * MSG), NW * MSG)
        prev = None
        for cl in range(COLS):
            o = out[cl * NW : (cl + 1) * NW]
            acc[pl.ds(start + 2 * cl, NW, stride=MSG), :] = o[:, :128]
            acc[pl.ds(start + 2 * cl + 1, NW, stride=MSG), :] = o[:, 128:256]
            if cl % 2 == 0:
                prev = o[:, 256:384]
            if cl % 2 == 1 or cl == COLS - 1:
                acc[pl.ds(start + 10 + cl // 2, NW, stride=MSG), :] = jnp.where(
                    lane64 < 64, prev, o[:, 256:384]
                )
        out1[pl.ds(gg * NW, NW)] = (
            acc[pl.ds(start, NW * MSG), :].reshape(NW, MSG, 128).astype(BF16)
        )

        @pl.when(i == 0)
        def _():
            pl.semaphore_wait(ready, 15)
            for copy in ocean_copies():
                copy.start()
            in1[me] = out1[me]

        def send(j, c):
            there = lax.rem(w + j, NW)
            pltpu.make_async_remote_copy(
                src_ref=out1.at[gg * NW + there, pl.ds(0, SENT)],
                dst_ref=in1.at[me, pl.ds(0, SENT)],
                send_sem=send1,
                recv_sem=recv1,
                device_id=(gg, there),
                device_id_type=MESH,
            ).start()
            return c

        lax.fori_loop(jnp.where(i == 0, 1, 0), NW, send, 0)
        return c

    lax.fori_loop(0, NG, make_group, 0)

    for copy in ocean_copies():
        copy.wait()
    sub_e = lax.broadcasted_iota(jnp.int32, (EXT, 256), 0)
    lane_e = lanes((EXT, 256))
    inside_rows = jnp.logical_and(
        jnp.logical_or(sub_e >= HALO, g > 0),
        jnp.logical_or(sub_e < HALO + OX, g < NG - 1),
    )
    inside = jnp.logical_and(
        inside_rows,
        jnp.logical_and(
            jnp.logical_or(lane_e < 252, w > 0),
            jnp.logical_or(jnp.logical_or(lane_e < 128, lane_e >= 252), w < NW - 1),
        ),
    )
    lane_m = lanes((EXT, 128))
    for k in range(FIELDS):
        ext[k, :HALO, :128] = in_rows[0, k]
        ext[k, HALO : HALO + OX, :128] = edge[k]
        ext[k, HALO + OX :, :128] = in_rows[1, k]
        from_left = pltpu.roll(in_slab[0], (124 - 4 * k) % 128, 1)
        from_right = pltpu.roll(in_slab[1], (128 - 4 * k) % 128, 1) if k else in_slab[1]
        ext[k, :, 128:] = jnp.where(
            lane_m >= 124, from_left, jnp.where(lane_m < 4, from_right, 0.0)
        )
    e_mask = jnp.where(inside, ext[OLEV], 0.0)
    ext[OLEV] = e_mask
    for k in range(2):
        ext[OLEV + 1 + k] = jnp.where(inside, ext[OLEV + 1 + k], 0.0)

    def level(k, c):
        cur = jnp.where(inside, ext[k], 0.0)
        add = jnp.where(k == 0, 1.0, 0.0).astype(F32) * ext[OLEV + 2]
        for _ in range(SWEEPS):
            lap = (
                pltpu.roll(cur, EXT - 1, 0)
                + pltpu.roll(cur, 1, 0)
                + pltpu.roll(cur, 255, 1)
                + pltpu.roll(cur, 1, 1)
                - 4.0 * cur
            )
            cur = ext[OLEV] * (cur + ext[OLEV + 1] * lap + add)
        ocean[k] = cur[HALO : HALO + OX, :128]
        return c

    lax.fori_loop(0, OLEV, level, 0)

    sub_p = lax.broadcasted_iota(jnp.int32, (128, 128), 0)
    lane_p = lanes((128, 128))
    upper = jnp.logical_and(sub_p < lane_p, sub_p // PAIRS == lane_p // PAIRS).astype(BF16)
    hits = p_dest[...] == w
    rank_in = jnp.dot(hits.astype(BF16), upper, preferred_element_type=F32)
    lane_h = lanes((NW // 2, 128))
    dst_in = p_dst[...].astype(F32) + 1.0
    pick_in = {}
    for half in range(2):
        mine = jnp.logical_and(hits, lane_h // PAIRS == half)
        for s in range(2):
            chosen_s = jnp.logical_and(mine, rank_in == float(s))
            row_of = jnp.sum(jnp.where(chosen_s, dst_in, 0.0), axis=1, keepdims=True)
            pick_in[half, s] = (lane_h.astype(F32) + 1.0 == row_of).astype(F32)

    def my_row(ref):
        row = ref[pl.ds(w // 2, 1), :]
        return jnp.where(lax.rem(w, 2) == 1, pltpu.roll(row, PAIRS, 1), row)[:, :PAIRS]

    my_dest = my_row(p_dest)
    my_src = my_row(p_src)
    same = lax.broadcasted_iota(jnp.int32, (NW, PAIRS), 0) == my_dest
    counts = jnp.dot(
        same.astype(BF16), upper[:PAIRS, :PAIRS], preferred_element_type=F32
    )
    rank_out = jnp.sum(jnp.where(same, counts, 0.0), axis=0, keepdims=True)
    pick_out = [
        jnp.logical_and(same, rank_out == float(s)).astype(F32) for s in range(2)
    ]
    src_row = my_src // 10
    seg_at = (my_src - src_row * 10) * 16 + src_row
    pick_seg = (lax.broadcasted_iota(jnp.int32, (160, PAIRS), 0) == seg_at).astype(BF16)

    degree = lanes((NLEV, WAVES))
    base = (degree * (degree + 1)).astype(F32) / float(WAVES * WAVES)
    rate = down(rates[...])
    weight = down(weights[...])
    damping = 1.0 / (1.0 + jnp.concatenate([rate] * 5, axis=1) * base)
    leg_copy.wait()

    def all_but_one(send_sem, recv_sem, src, dst):
        return pltpu.make_async_remote_copy(
            src_ref=src.at[pl.ds(0, ND - 1), pl.ds(0, SENT)],
            dst_ref=dst.at[pl.ds(0, ND - 1), pl.ds(0, SENT)],
            send_sem=send_sem,
            recv_sem=recv_sem,
            device_id=(g, w),
            device_id_type=MESH,
        )

    def widen(src):
        def step(i, c):
            n = ND // 16
            acc[pl.ds(pl.multiple_of(i * n * MSG, n * MSG), n * MSG), :] = (
                src[pl.ds(i * n, n)].astype(F32).reshape(n * MSG, 128)
            )
            return c

        lax.fori_loop(0, 16, step, 0)

    first = all_but_one(send1, recv1, out1, in1)
    first.wait_send()
    first.wait_recv()
    widen(in1)

    def at(ref, start, n, stride):
        return ref[pl.ds(start, n, stride=stride), :]

    for cl in range(COLS):
        for t in range(2):
            v = [at(acc, k * NW * MSG + 2 * cl + t, NW, MSG) for k in range(NG)]
            for q, out in enumerate(swap_blocks(v, lane64)):
                cols_f[pl.ds(cl * WAVES + 4 * t + q, NW, stride=ROWS), :] = out
    for p in range(3):
        v = [at(acc, k * NW * MSG + 10 + p, NW, MSG) for k in range(NG)]
        for q, out in enumerate(swap_blocks(v, lane64)):
            if 2 * p + q // 2 < COLS:
                cols_f[pl.ds((2 * p + q // 2) * WAVES + 8 + q % 2, NW, stride=ROWS), :] = out

    odd = lax.rem(g, 2)

    def column(cl, c):
        here = pl.ds(pl.multiple_of(cl * WAVES, WAVES), WAVES)
        table_of = leg[(odd + cl) // 2]
        m = wos_s[w * 10 + (COLS * g + cl) // 2]
        spectra = jnp.dot(
            cols_f[here, :].T.astype(BF16), table_of, preferred_element_type=F32
        )
        spectra = jnp.where(degree >= m, spectra, 0.0).astype(BF16)
        modal = jnp.dot(analysis[...], spectra, preferred_element_type=F32)
        modal = (modal * damping).astype(BF16)
        solved = jnp.dot(synthesis[...], modal, preferred_element_type=F32).astype(BF16)
        flux_coef = jnp.concatenate(
            [
                jnp.sum(
                    weight * solved[:, b * 128 : (b + 1) * 128].astype(F32),
                    axis=0,
                    keepdims=True,
                )
                for b in range(5)
            ],
            axis=1,
        )
        right = jnp.concatenate(
            [solved, jnp.broadcast_to(flux_coef, (128, WAVES)).astype(BF16)], axis=0
        )
        back = nt(table_of, right)
        cols_f[here, :] = back[:, :128]
        flux_f[here, :] = back[:, 128:]
        return c

    lax.fori_loop(0, COLS, column, 0)

    for cl in range(COLS):
        for t in range(2):
            v = [at(cols_f, cl * WAVES + 4 * t + q, NW, ROWS) for q in range(NG)]
            for k, out in enumerate(swap_blocks(v, lane64)):
                acc[pl.ds(k * NW * MSG + 2 * cl + t, NW, stride=MSG), :] = out
    fluxes = jnp.zeros((NW, 128), F32)
    for cl in range(COLS):
        for r in range(ROWS):
            fluxes = jnp.where(
                lane64 == 64 + cl * ROWS + r, at(flux_f, cl * WAVES + r, NW, ROWS), fluxes
            )
    for p in range(3):
        v = []
        for q in range(4):
            cl = min(2 * p + q // 2, COLS - 1)
            v.append(at(cols_f, cl * WAVES + 8 + q % 2, NW, ROWS))
        for k, out in enumerate(swap_blocks(v, lane64)):
            if p == 2:
                out = jnp.where(lane64 < 64, out, fluxes)
            acc[pl.ds(k * NW * MSG + 10 + p, NW, stride=MSG), :] = out

    def send_group(i, c):
        gg = lax.rem(g + i, NG)
        start = pl.multiple_of(gg * (NW * MSG), NW * MSG)
        out1[pl.ds(gg * NW, NW)] = (
            acc[pl.ds(start, NW * MSG), :].reshape(NW, MSG, 128).astype(BF16)
        )

        @pl.when(i == 0)
        def _():
            in2[me] = out1[me]

        def send(j, c):
            there = lax.rem(w + j, NW)
            pltpu.make_async_remote_copy(
                src_ref=out1.at[gg * NW + there, pl.ds(0, SENT)],
                dst_ref=in2.at[me, pl.ds(0, SENT)],
                send_sem=send2,
                recv_sem=recv2,
                device_id=(gg, there),
                device_id_type=MESH,
            ).start()
            return c

        lax.fori_loop(jnp.where(i == 0, 1, 0), NW, send, 0)
        return c

    lax.fori_loop(0, NG, send_group, 0)
    mats_copy.wait()
    second = all_but_one(send2, recv2, out1, in2)
    second.wait_send()
    second.wait_recv()
    widen(in2)

    for k in range(NG):
        f12 = at(acc, k * NW * MSG + 12, NW, MSG)
        for cl in range(COLS):
            rows = pl.ds((k * COLS + cl) * NW, NW)
            for t in range(2):
                lhs[rows, t * 128 : (t + 1) * 128] = at(
                    acc, k * NW * MSG + 2 * cl + t, NW, MSG
                ).astype(BF16)
            v = at(acc, k * NW * MSG + 10 + cl // 2, NW, MSG) if cl < 4 else f12
            if cl % 2 == 1:
                v = pltpu.roll(v, 64, 1)
            f = pltpu.roll(f12, 128 - cl * ROWS, 1) if cl else f12
            lhs[rows, 256:384] = jnp.where(
                lane64 < 64, v, jnp.where(lane64 < 64 + ROWS, f, 0.0)
            ).astype(BF16)
    last = tn(lhs[:, 256:384], table[...])
    mu = [
        -cos_turns(jnp.full((LEV, 128), lat_s[r], jnp.int32).astype(F32) + 0.5, 1.0)
        for r in range(ROWS)
    ]

    def finish(r, grid):
        for jt in range(10):
            cut = slice(jt * 128, (jt + 1) * 128)
            atm[r, :, cut] = (
                grid[:, cut] * (1.0 + field[r, :, cut].astype(F32) * mu[r])
            ).astype(BF16)

    for jt in range(10):
        segs[jt * 16 : (jt + 1) * 16, :] = last[64:80, jt * 128 : (jt + 1) * 128].astype(BF16)
    chosen = tn(pick_seg, segs[...]).astype(BF16)
    sub8 = lax.broadcasted_iota(jnp.int32, (8, 128), 0)
    parts = []
    for b in range(PAIRS // 8):
        total = jnp.zeros((8, 128), F32)
        eight = chosen[b * 8 : (b + 1) * 8]
        for u in range(8):
            total = jnp.where(sub8 == u, nt(eight, mats_v[b * 8 + u]), total)
        parts.append(total)
    products = jnp.concatenate(parts, axis=0)
    for s in range(2):
        out3[pl.ds(s, NW, stride=8), :] = jnp.dot(
            pick_out[s], products, precision=HIGH, preferred_element_type=F32
        )
    in3[pl.ds(pl.multiple_of(w * 8, 8), 8), :] = out3[pl.ds(pl.multiple_of(w * 8, 8), 8), :]

    def send_flux(j, c):
        there = lax.rem(w + j, NW)
        pltpu.make_async_remote_copy(
            src_ref=out3.at[pl.ds(pl.multiple_of(there * 8, 8), 8)],
            dst_ref=in3.at[pl.ds(pl.multiple_of(w * 8, 8), 8)],
            send_sem=send3,
            recv_sem=recv3,
            device_id=(g, there),
            device_id_type=MESH,
        ).start()
        return c

    lax.fori_loop(1, NW, send_flux, 0)

    for r in range(2):
        finish(8 + r, last[r * LEV : (r + 1) * LEV])
    for t in range(2):
        main = tn(lhs[:, t * 128 : (t + 1) * 128], table[...])
        for q in range(4):
            finish(4 * t + q, main[q * LEV : (q + 1) * LEV])

    third = pltpu.make_async_remote_copy(
        src_ref=out3.at[pl.ds(0, (NW - 1) * 8)],
        dst_ref=in3.at[pl.ds(0, (NW - 1) * 8)],
        send_sem=send3,
        recv_sem=recv3,
        device_id=(g, w),
        device_id_type=MESH,
    )
    third.wait_send()
    third.wait_recv()
    summed = jnp.zeros((128, 128), F32)
    for half in range(2):
        for s in range(2):
            summed = summed + tn(
                pick_in[half, s], at(in3, half * 8 + s, NW // 2, 16), HIGH
            )
    flux[...] = summed[:OX]


def hand_over(atm_in, ocean_in, flux_in, atm, ocean, flux, atm_v, ocean_v, flux_v, came, went):
    parts = [(atm_in.at[r], atm_v.at[r], atm.at[r]) for r in range(ROWS)]
    parts += [(ocean_in, ocean_v, ocean), (flux_in, flux_v, flux)]
    ins = [pltpu.make_async_copy(a, v, came.at[i]) for i, (a, v, _) in enumerate(parts)]
    outs = [pltpu.make_async_copy(v, b, went.at[i]) for i, (_, v, b) in enumerate(parts)]
    for copy in ins:
        copy.start()
    for come, go in zip(ins, outs):
        come.wait()
        go.start()
    for copy in outs:
        copy.wait()


def per_device(
    grid_field,
    legendre,
    wave_of_slot,
    lat_of_row,
    analysis,
    synthesis,
    mode_rates,
    flux_weights,
    remap_mats,
    pair_dest,
    pair_src,
    pair_dst,
    ocean_temp,
    diffusivity,
    surface_heat,
    land_mask,
):
    smem = pl.BlockSpec(memory_space=pltpu.SMEM)
    vmem = pl.BlockSpec(memory_space=pltpu.VMEM)
    anys = pl.BlockSpec(memory_space=pl.ANY)
    atm, ocean, flux = pl.pallas_call(
        kernel,
        out_shape=(
            jax.ShapeDtypeStruct((ROWS, LEV, LON), BF16),
            jax.ShapeDtypeStruct((OLEV, OX, 128), F32),
            jax.ShapeDtypeStruct((OX, 128), F32),
        ),
        in_specs=[smem, smem, vmem, anys, vmem, vmem, vmem, vmem, vmem, anys]
        + [vmem] * 7,
        out_specs=(vmem, vmem, vmem),
        scratch_shapes=[
            pltpu.VMEM((LON, LON), BF16),
            pltpu.VMEM((384, LON), BF16),
            pltpu.VMEM((10, NW, 128), F32),
            pltpu.VMEM((ND * MSG, 128), F32),
            pltpu.VMEM((ND, MSG, 128), BF16),
            pltpu.VMEM((ND, MSG, 128), BF16),
            pltpu.VMEM((ND, MSG, 128), BF16),
            pltpu.VMEM((SLOTS, WAVES, WAVES), BF16),
            pltpu.VMEM((COLS * WAVES, 128), F32),
            pltpu.VMEM((COLS * WAVES, 128), F32),
            pltpu.VMEM((LON, 384), BF16),
            pltpu.VMEM((160, 128), BF16),
            pltpu.VMEM((PAIRS, 128, 128), BF16),
            pltpu.VMEM((NW * 8, 128), F32),
            pltpu.VMEM((NW * 8, 128), F32),
            pltpu.VMEM((FIELDS, OX, 128), F32),
            pltpu.VMEM((2, FIELDS, HALO, 128), F32),
            pltpu.VMEM((2, FIELDS, HALO, 128), F32),
            pltpu.VMEM((2, OX, 128), F32),
            pltpu.VMEM((2, EXT, 128), F32),
            pltpu.VMEM((FIELDS, EXT, 256), F32),
            pltpu.SemaphoreType.REGULAR,
            pltpu.SemaphoreType.DMA((2,)),
            pltpu.SemaphoreType.DMA(()),
            pltpu.SemaphoreType.DMA(()),
            pltpu.SemaphoreType.DMA(()),
            pltpu.SemaphoreType.DMA(()),
            pltpu.SemaphoreType.DMA(()),
            pltpu.SemaphoreType.DMA(()),
            pltpu.SemaphoreType.DMA((8,)),
            pltpu.SemaphoreType.DMA((8,)),
        ],
        compiler_params=pltpu.CompilerParams(
            collective_id=0, has_side_effects=True, vmem_limit_bytes=60 * 1024 * 1024
        ),
        name="step",
    )(
        wave_of_slot,
        lat_of_row,
        grid_field.transpose(1, 0, 2),
        legendre,
        wave_of_slot,
        analysis,
        synthesis,
        mode_rates.reshape(1, NLEV),
        flux_weights.reshape(1, NLEV),
        remap_mats,
        pair_dest.reshape(NW // 2, 128),
        pair_src.reshape(NW // 2, 128),
        pair_dst.reshape(NW // 2, 128),
        ocean_temp,
        diffusivity,
        surface_heat,
        land_mask,
    )
    atm, ocean, flux = pl.pallas_call(
        hand_over,
        out_shape=tuple(jax.ShapeDtypeStruct(v.shape, v.dtype) for v in (atm, ocean, flux)),
        in_specs=[anys] * 3,
        out_specs=(anys,) * 3,
        scratch_shapes=[
            pltpu.VMEM((ROWS, LEV, LON), BF16),
            pltpu.VMEM((OLEV, OX, 128), F32),
            pltpu.VMEM((OX, 128), F32),
            pltpu.SemaphoreType.DMA((ROWS + 2,)),
            pltpu.SemaphoreType.DMA((ROWS + 2,)),
        ],
        name="hand_over",
    )(atm, ocean, flux)
    return atm.transpose(1, 0, 2), ocean, flux


def solution(mesh):
    return jax.shard_map(
        per_device,
        mesh=mesh,
        in_specs=(
            P("lev", "wav", None),
            P("wav", None, None),
            P(),
            P("wav"),
            P(),
            P(),
            P(),
            P(),
            P("lev", "wav", None, None),
            P("lev", None, None),
            P("lev", None),
            P("lev", None),
            P(None, "lev", "wav"),
            P("lev", "wav"),
            P("lev", "wav"),
            P("lev", "wav"),
        ),
        out_specs=(P("lev", "wav", None), P(None, "lev", "wav"), P("lev", "wav")),
        check_vma=False,
    )
```

```python
import functools
import math

import jax
import jax.numpy as jnp
from jax import lax
from jax.experimental import pallas as pl
from jax.experimental.pallas import tpu as pltpu
from jax.sharding import PartitionSpec as P

MESH = pl.DeviceIdType.MESH
F32 = jnp.float32
BF16 = jnp.bfloat16
HIGH = lax.Precision.HIGHEST

SWEEPS = 4
NG = 4
NW = 64
ND = NG * NW
LEV = 32
ROWS = 10
LON = 1280
WAVES = 640
NLEV = 128
COLS = 5
SLOTS = 3
MSG = 16
SENT = 14
PAIRS = 64
OX = 48
OLEV = 8
HALO = 8
EXT = OX + 2 * HALO
FIELDS = OLEV + 3

SIN_POLY = (6.28318528, -41.34168068, 81.60248108, -76.58128818, 39.76072297)


def nt(a, b):
    return lax.dot_general(a, b, (((1,), (1,)), ((), ())), preferred_element_type=F32)


def tn(a, b, precision=None):
    return lax.dot_general(
        a, b, (((0,), (0,)), ((), ())), preferred_element_type=F32, precision=precision
    )


def cos_turns(phase, scale):
    whole = jnp.floor(phase * (1.0 / LON) + 0.5)
    rest = jnp.abs(phase - whole * LON)
    t = (LON / 4 - rest) * (1.0 / LON)
    z = t * t
    c = [scale * v for v in SIN_POLY]
    return t * (c[0] + z * (c[1] + z * (c[2] + z * (c[3] + z * c[4]))))


def swap_blocks(v, lane):
    low = lane < 64
    even = lax.rem(lane // 32, 2) == 0
    a0 = jnp.where(low, v[0], pltpu.roll(v[2], 64, 1))
    a2 = jnp.where(low, pltpu.roll(v[0], 64, 1), v[2])
    a1 = jnp.where(low, v[1], pltpu.roll(v[3], 64, 1))
    a3 = jnp.where(low, pltpu.roll(v[1], 64, 1), v[3])
    return (
        jnp.where(even, a0, pltpu.roll(a1, 32, 1)),
        jnp.where(even, pltpu.roll(a0, 96, 1), a1),
        jnp.where(even, a2, pltpu.roll(a3, 32, 1)),
        jnp.where(even, pltpu.roll(a2, 96, 1), a3),
    )


def lanes(shape):
    return lax.broadcasted_iota(jnp.int32, shape, len(shape) - 1)


def down(row):
    return jnp.broadcast_to(row, (128, 128)).T


def kernel(
    wos_s,
    lat_s,
    field_in,
    legendre,
    wos_v,
    analysis,
    synthesis,
    rates,
    weights,
    mats,
    p_dest,
    p_src,
    p_dst,
    temp,
    kappa,
    heat,
    mask,
    atm,
    ocean,
    flux,
    field,
    table,
    rows_in,
    waves,
    acc,
    out1,
    in1,
    in2,
    leg,
    cols_f,
    flux_f,
    lhs,
    segs,
    mats_v,
    out3,
    in3,
    edge,
    rows_edge,
    in_rows,
    slab,
    in_slab,
    ext,
    ready,
    local_sem,
    send1,
    recv1,
    send2,
    recv2,
    send3,
    recv3,
    send4,
    recv4,
):
    g = lax.axis_index("lev")
    w = lax.axis_index("wav")
    me = g * NW + w
    barrier = pltpu.get_barrier_semaphore()
    out3_rows = out3.reshape(NW * 8, 128)
    in3_rows = in3.reshape(NW * 8, 128)

    field_copy = pltpu.make_async_copy(field_in, field, local_sem.at[2])
    field_copy.start()
    first_slot = (COLS * g) // 2
    leg_copy = pltpu.make_async_copy(
        legendre.at[pl.ds(first_slot, SLOTS)], leg, local_sem.at[0]
    )
    leg_copy.start()
    mats_copy = pltpu.make_async_copy(mats.at[0], mats_v, local_sem.at[1])
    mats_copy.start()

    outer, inner = w // 8, lax.rem(w, 8)
    far = [(g, lax.rem(outer + j, 8) * 8 + inner) for j in range(1, 8)]
    near = [(g, outer * 8 + lax.rem(inner + j, 8)) for j in range(1, 8)]
    across = [(lax.rem(g + j, NG), w) for j in range(1, NG)]

    def tell(sem, partners):
        for partner in partners:
            pl.semaphore_signal(sem, inc=1, device_id=partner, device_id_type=MESH)

    tell(barrier, far + near + across)
    field_copy.wait()

    for r in range(ROWS):
        rows_in[r * LEV : (r + 1) * LEV, :] = field[r]
    rows_in[320:352, :] = field[8]
    rows_in[352:384, :] = field[9]

    sub_w = lax.broadcasted_iota(jnp.int32, (NW, WAVES), 0)
    at_slot = lanes((NW, WAVES)) - 10 * sub_w
    all_waves = jnp.broadcast_to(wos_v[...].reshape(1, WAVES).astype(F32), (NW, WAVES))
    for k in range(10):
        m = jnp.sum(jnp.where(at_slot == k, all_waves, 0.0), axis=1, keepdims=True)
        waves[k] = jnp.broadcast_to(m, (NW, 128))

    ocean_mask = mask[...].astype(F32)
    for k in range(OLEV):
        edge[k] = temp[k] * ocean_mask
    edge[OLEV] = ocean_mask
    edge[OLEV + 1] = kappa[...]
    edge[OLEV + 2] = heat[...]
    lane48 = lanes((OX, 128))
    left = jnp.zeros((OX, 128), F32)
    right = jnp.zeros((OX, 128), F32)
    for k in range(FIELDS):
        here = lane48 // 4 == k
        v = edge[k]
        left = jnp.where(here, pltpu.roll(v, 4 * k, 1) if k else v, left)
        right = jnp.where(here, pltpu.roll(v, (4 * k + 4) % 128, 1), right)
        rows_edge[0, k] = v[:HALO]
        rows_edge[1, k] = v[OX - HALO :]
    slab[0] = left
    slab[1] = right

    up, dn = lax.rem(g + NG - 1, NG), lax.rem(g + 1, NG)
    wl, wr = lax.rem(w + NW - 1, NW), lax.rem(w + 1, NW)

    def ocean_copies():
        c = []
        c.append((rows_edge.at[0], in_rows.at[1], (up, w)))
        c.append((rows_edge.at[1], in_rows.at[0], (dn, w)))
        for side, ww in ((0, wl), (1, wr)):
            c.append((slab.at[side], in_slab.at[1 - side, pl.ds(HALO, OX)], (g, ww)))
            c.append(
                (slab.at[side, pl.ds(0, HALO)], in_slab.at[1 - side, pl.ds(HALO + OX, HALO)], (up, ww))
            )
            c.append(
                (slab.at[side, pl.ds(OX - HALO, HALO)], in_slab.at[1 - side, pl.ds(0, HALO)], (dn, ww))
            )
        return [
            pltpu.make_async_remote_copy(
                src_ref=s, dst_ref=d, send_sem=send4.at[i], recv_sem=recv4.at[i],
                device_id=dev, device_id_type=MESH,
            )
            for i, (s, d, dev) in enumerate(c)
        ]

    lane64 = lanes((NW, 128))
    pl.semaphore_wait(barrier, len(far) + len(near) + len(across))
    tell(ready.at[0], near)

    def make_group(i, c):
        gg = lax.rem(g + i, NG)
        base = pl.multiple_of(gg * (COLS * NW), NW)
        for cl in range(COLS):
            q = gg * COLS + cl
            m = waves[q // 2]
            shift = (lax.rem(q, 2) * (LON // 4)).astype(F32)
            scale = math.sqrt(2.0 / LON)
            phase = m * lane64.astype(F32) + shift
            now = cos_turns(phase, scale)
            before = cos_turns(phase - 128.0 * m, scale)
            twice = cos_turns(128.0 * m, 2.0)
            for a in range(10):
                table[pl.ds(base + cl * NW, NW), a * 128 : (a + 1) * 128] = now.astype(BF16)
                now, before = twice * now - before, now
        @pl.when(i == 0)
        def _():
            pl.semaphore_wait(ready.at[0], len(near))
            tell(ready.at[1], across)

        out = nt(table[pl.ds(base, COLS * NW), :], rows_in[...])
        start = pl.multiple_of(gg * (NW * MSG), NW * MSG)
        prev = None
        for cl in range(COLS):
            o = out[cl * NW : (cl + 1) * NW]
            acc[pl.ds(start + 2 * cl, NW, stride=MSG), :] = o[:, :128]
            acc[pl.ds(start + 2 * cl + 1, NW, stride=MSG), :] = o[:, 128:256]
            if cl % 2 == 0:
                prev = o[:, 256:384]
            if cl % 2 == 1 or cl == COLS - 1:
                acc[pl.ds(start + 10 + cl // 2, NW, stride=MSG), :] = jnp.where(
                    lane64 < 64, prev, o[:, 256:384]
                )
        out1[pl.ds(gg * NW, NW)] = (
            acc[pl.ds(start, NW * MSG), :].reshape(NW, MSG, 128).astype(BF16)
        )

        @pl.when(i == 0)
        def _():
            pl.semaphore_wait(ready.at[1], len(across))
            for copy in ocean_copies():
                copy.start()
            in1[me] = out1[me]

        def send(j, c):
            there = lax.rem(w + j, NW)
            pltpu.make_async_remote_copy(
                src_ref=out1.at[gg * NW + there, pl.ds(0, SENT)],
                dst_ref=in1.at[me, pl.ds(0, SENT)],
                send_sem=send1,
                recv_sem=recv1,
                device_id=(gg, there),
                device_id_type=MESH,
            ).start()
            return c

        lax.fori_loop(jnp.where(i == 0, 1, 0), NW, send, 0)
        return c

    lax.fori_loop(0, NG, make_group, 0)

    for copy in ocean_copies():
        copy.wait()
    sub_e = lax.broadcasted_iota(jnp.int32, (EXT, 256), 0)
    lane_e = lanes((EXT, 256))
    inside_rows = jnp.logical_and(
        jnp.logical_or(sub_e >= HALO, g > 0),
        jnp.logical_or(sub_e < HALO + OX, g < NG - 1),
    )
    inside = jnp.logical_and(
        inside_rows,
        jnp.logical_and(
            jnp.logical_or(lane_e < 252, w > 0),
            jnp.logical_or(jnp.logical_or(lane_e < 128, lane_e >= 252), w < NW - 1),
        ),
    )
    lane_m = lanes((EXT, 128))
    for k in range(FIELDS):
        ext[k, :HALO, :128] = in_rows[0, k]
        ext[k, HALO : HALO + OX, :128] = edge[k]
        ext[k, HALO + OX :, :128] = in_rows[1, k]
        from_left = pltpu.roll(in_slab[0], (124 - 4 * k) % 128, 1)
        from_right = pltpu.roll(in_slab[1], (128 - 4 * k) % 128, 1) if k else in_slab[1]
        ext[k, :, 128:] = jnp.where(
            lane_m >= 124, from_left, jnp.where(lane_m < 4, from_right, 0.0)
        )
    e_mask = jnp.where(inside, ext[OLEV], 0.0)
    ext[OLEV] = e_mask
    for k in range(2):
        ext[OLEV + 1 + k] = jnp.where(inside, ext[OLEV + 1 + k], 0.0)

    def level(k, c):
        cur = jnp.where(inside, ext[k], 0.0)
        add = jnp.where(k == 0, 1.0, 0.0).astype(F32) * ext[OLEV + 2]
        for _ in range(SWEEPS):
            lap = (
                pltpu.roll(cur, EXT - 1, 0)
                + pltpu.roll(cur, 1, 0)
                + pltpu.roll(cur, 255, 1)
                + pltpu.roll(cur, 1, 1)
                - 4.0 * cur
            )
            cur = ext[OLEV] * (cur + ext[OLEV + 1] * lap + add)
        ocean[k] = cur[HALO : HALO + OX, :128]
        return c

    lax.fori_loop(0, OLEV, level, 0)

    sub_p = lax.broadcasted_iota(jnp.int32, (128, 128), 0)
    lane_p = lanes((128, 128))
    upper = jnp.logical_and(sub_p < lane_p, sub_p // PAIRS == lane_p // PAIRS).astype(BF16)
    hits = p_dest[...] == w
    rank_in = jnp.dot(hits.astype(BF16), upper, preferred_element_type=F32)
    lane_h = lanes((NW // 2, 128))
    dst_in = p_dst[...].astype(F32) + 1.0
    pick_in = {}
    for half in range(2):
        mine = jnp.logical_and(hits, lane_h // PAIRS == half)
        for s in range(2):
            chosen_s = jnp.logical_and(mine, rank_in == float(s))
            row_of = jnp.sum(jnp.where(chosen_s, dst_in, 0.0), axis=1, keepdims=True)
            pick_in[half, s] = (lane_h.astype(F32) + 1.0 == row_of).astype(F32)

    def my_row(ref):
        row = ref[pl.ds(w // 2, 1), :]
        return jnp.where(lax.rem(w, 2) == 1, pltpu.roll(row, PAIRS, 1), row)[:, :PAIRS]

    my_dest = my_row(p_dest)
    my_src = my_row(p_src)
    same = lax.broadcasted_iota(jnp.int32, (NW, PAIRS), 0) == my_dest
    counts = jnp.dot(
        same.astype(BF16), upper[:PAIRS, :PAIRS], preferred_element_type=F32
    )
    rank_out = jnp.sum(jnp.where(same, counts, 0.0), axis=0, keepdims=True)
    pick_out = [
        jnp.logical_and(same, rank_out == float(s)).astype(F32) for s in range(2)
    ]
    src_row = my_src // 10
    seg_at = (my_src - src_row * 10) * 16 + src_row
    pick_seg = (lax.broadcasted_iota(jnp.int32, (160, PAIRS), 0) == seg_at).astype(BF16)

    degree = lanes((NLEV, WAVES))
    base = (degree * (degree + 1)).astype(F32) / float(WAVES * WAVES)
    rate = down(rates[...])
    weight = down(weights[...])
    damping = 1.0 / (1.0 + jnp.concatenate([rate] * 5, axis=1) * base)
    leg_copy.wait()

    def all_but_one(send_sem, recv_sem, src, dst):
        return pltpu.make_async_remote_copy(
            src_ref=src.at[pl.ds(0, ND - 1), pl.ds(0, SENT)],
            dst_ref=dst.at[pl.ds(0, ND - 1), pl.ds(0, SENT)],
            send_sem=send_sem,
            recv_sem=recv_sem,
            device_id=(g, w),
            device_id_type=MESH,
        )

    def widen(src):
        def step(i, c):
            n = ND // 16
            acc[pl.ds(pl.multiple_of(i * n * MSG, n * MSG), n * MSG), :] = (
                src[pl.ds(i * n, n)].astype(F32).reshape(n * MSG, 128)
            )
            return c

        lax.fori_loop(0, 16, step, 0)

    first = all_but_one(send1, recv1, out1, in1)
    first.wait_send()
    first.wait_recv()
    widen(in1)

    def at(ref, start, n, stride):
        return ref[pl.ds(start, n, stride=stride), :]

    for cl in range(COLS):
        for t in range(2):
            v = [at(acc, k * NW * MSG + 2 * cl + t, NW, MSG) for k in range(NG)]
            for q, out in enumerate(swap_blocks(v, lane64)):
                cols_f[pl.ds(cl * WAVES + 4 * t + q, NW, stride=ROWS), :] = out
    for p in range(3):
        v = [at(acc, k * NW * MSG + 10 + p, NW, MSG) for k in range(NG)]
        for q, out in enumerate(swap_blocks(v, lane64)):
            if 2 * p + q // 2 < COLS:
                cols_f[pl.ds((2 * p + q // 2) * WAVES + 8 + q % 2, NW, stride=ROWS), :] = out

    odd = lax.rem(g, 2)

    def column(cl, c):
        here = pl.ds(pl.multiple_of(cl * WAVES, WAVES), WAVES)
        table_of = leg[(odd + cl) // 2]
        m = wos_s[w * 10 + (COLS * g + cl) // 2]
        spectra = jnp.dot(
            cols_f[here, :].T.astype(BF16), table_of, preferred_element_type=F32
        )
        spectra = jnp.where(degree >= m, spectra, 0.0).astype(BF16)
        modal = jnp.dot(analysis[...], spectra, preferred_element_type=F32)
        modal = (modal * damping).astype(BF16)
        solved = jnp.dot(synthesis[...], modal, preferred_element_type=F32).astype(BF16)
        flux_coef = jnp.concatenate(
            [
                jnp.sum(
                    weight * solved[:, b * 128 : (b + 1) * 128].astype(F32),
                    axis=0,
                    keepdims=True,
                )
                for b in range(5)
            ],
            axis=1,
        )
        right = jnp.concatenate(
            [solved, jnp.broadcast_to(flux_coef, (128, WAVES)).astype(BF16)], axis=0
        )
        back = nt(table_of, right)
        cols_f[here, :] = back[:, :128]
        flux_f[here, :] = back[:, 128:]
        return c

    lax.fori_loop(0, COLS, column, 0)

    for cl in range(COLS):
        for t in range(2):
            v = [at(cols_f, cl * WAVES + 4 * t + q, NW, ROWS) for q in range(NG)]
            for k, out in enumerate(swap_blocks(v, lane64)):
                acc[pl.ds(k * NW * MSG + 2 * cl + t, NW, stride=MSG), :] = out
    fluxes = jnp.zeros((NW, 128), F32)
    for cl in range(COLS):
        for r in range(ROWS):
            fluxes = jnp.where(
                lane64 == 64 + cl * ROWS + r, at(flux_f, cl * WAVES + r, NW, ROWS), fluxes
            )
    for p in range(3):
        v = []
        for q in range(4):
            cl = min(2 * p + q // 2, COLS - 1)
            v.append(at(cols_f, cl * WAVES + 8 + q % 2, NW, ROWS))
        for k, out in enumerate(swap_blocks(v, lane64)):
            if p == 2:
                out = jnp.where(lane64 < 64, out, fluxes)
            acc[pl.ds(k * NW * MSG + 10 + p, NW, stride=MSG), :] = out

    def send_group(i, c):
        gg = lax.rem(g + i, NG)
        start = pl.multiple_of(gg * (NW * MSG), NW * MSG)
        out1[pl.ds(gg * NW, NW)] = (
            acc[pl.ds(start, NW * MSG), :].reshape(NW, MSG, 128).astype(BF16)
        )

        @pl.when(i == 0)
        def _():
            in2[me] = out1[me]

        def send(j, c):
            there = lax.rem(w + j, NW)
            pltpu.make_async_remote_copy(
                src_ref=out1.at[gg * NW + there, pl.ds(0, SENT)],
                dst_ref=in2.at[me, pl.ds(0, SENT)],
                send_sem=send2,
                recv_sem=recv2,
                device_id=(gg, there),
                device_id_type=MESH,
            ).start()
            return c

        lax.fori_loop(jnp.where(i == 0, 1, 0), NW, send, 0)
        return c

    lax.fori_loop(0, NG, send_group, 0)
    mats_copy.wait()
    second = all_but_one(send2, recv2, out1, in2)
    second.wait_send()
    second.wait_recv()
    widen(in2)

    for k in range(NG):
        f12 = at(acc, k * NW * MSG + 12, NW, MSG)
        for cl in range(COLS):
            rows = pl.ds((k * COLS + cl) * NW, NW)
            for t in range(2):
                lhs[rows, t * 128 : (t + 1) * 128] = at(
                    acc, k * NW * MSG + 2 * cl + t, NW, MSG
                ).astype(BF16)
            v = at(acc, k * NW * MSG + 10 + cl // 2, NW, MSG) if cl < 4 else f12
            if cl % 2 == 1:
                v = pltpu.roll(v, 64, 1)
            f = pltpu.roll(f12, 128 - cl * ROWS, 1) if cl else f12
            lhs[rows, 256:384] = jnp.where(
                lane64 < 64, v, jnp.where(lane64 < 64 + ROWS, f, 0.0)
            ).astype(BF16)
    last = tn(lhs[:, 256:384], table[...])
    mu = [
        -cos_turns(jnp.full((LEV, 128), lat_s[r], jnp.int32).astype(F32) + 0.5, 1.0)
        for r in range(ROWS)
    ]

    def finish(r, grid):
        for jt in range(10):
            cut = slice(jt * 128, (jt + 1) * 128)
            atm[r, :, cut] = (
                grid[:, cut] * (1.0 + field[r, :, cut].astype(F32) * mu[r])
            ).astype(BF16)

    for jt in range(10):
        segs[jt * 16 : (jt + 1) * 16, :] = last[64:80, jt * 128 : (jt + 1) * 128].astype(BF16)
    chosen = tn(pick_seg, segs[...]).astype(BF16)
    sub8 = lax.broadcasted_iota(jnp.int32, (8, 128), 0)
    parts = []
    for b in range(PAIRS // 8):
        total = jnp.zeros((8, 128), F32)
        eight = chosen[b * 8 : (b + 1) * 8]
        for u in range(8):
            total = jnp.where(sub8 == u, nt(eight, mats_v[b * 8 + u]), total)
        parts.append(total)
    products = jnp.concatenate(parts, axis=0)
    for s in range(2):
        out3_rows[pl.ds(s, NW, stride=8), :] = jnp.dot(
            pick_out[s], products, precision=HIGH, preferred_element_type=F32
        )
    in3[w] = out3[w]

    def send_flux(j, c):
        there = lax.rem(w + j, NW)
        pltpu.make_async_remote_copy(
            src_ref=out3.at[there, pl.ds(0, 2)],
            dst_ref=in3.at[w, pl.ds(0, 2)],
            send_sem=send3,
            recv_sem=recv3,
            device_id=(g, there),
            device_id_type=MESH,
        ).start()
        return c

    lax.fori_loop(1, NW, send_flux, 0)

    for r in range(2):
        finish(8 + r, last[r * LEV : (r + 1) * LEV])
    for t in range(2):
        main = tn(lhs[:, t * 128 : (t + 1) * 128], table[...])
        for q in range(4):
            finish(4 * t + q, main[q * LEV : (q + 1) * LEV])

    third = pltpu.make_async_remote_copy(
        src_ref=out3.at[pl.ds(0, NW - 1), pl.ds(0, 2)],
        dst_ref=in3.at[pl.ds(0, NW - 1), pl.ds(0, 2)],
        send_sem=send3,
        recv_sem=recv3,
        device_id=(g, w),
        device_id_type=MESH,
    )
    third.wait_send()
    third.wait_recv()
    summed = jnp.zeros((128, 128), F32)
    for half in range(2):
        for s in range(2):
            summed = summed + tn(
                pick_in[half, s], at(in3_rows, half * 8 + s, NW // 2, 16), HIGH
            )
    flux[...] = summed[:OX]


def hand_over(atm_in, ocean_in, flux_in, atm, ocean, flux, atm_v, ocean_v, flux_v, came, went):
    parts = [(atm_in.at[r], atm_v.at[r], atm.at[r]) for r in range(ROWS)]
    parts += [(ocean_in, ocean_v, ocean), (flux_in, flux_v, flux)]
    ins = [pltpu.make_async_copy(a, v, came.at[i]) for i, (a, v, _) in enumerate(parts)]
    outs = [pltpu.make_async_copy(v, b, went.at[i]) for i, (_, v, b) in enumerate(parts)]
    for copy in ins:
        copy.start()
    for come, go in zip(ins, outs):
        come.wait()
        go.start()
    for copy in outs:
        copy.wait()


def per_device(
    grid_field,
    legendre,
    wave_of_slot,
    lat_of_row,
    analysis,
    synthesis,
    mode_rates,
    flux_weights,
    remap_mats,
    pair_dest,
    pair_src,
    pair_dst,
    ocean_temp,
    diffusivity,
    surface_heat,
    land_mask,
):
    smem = pl.BlockSpec(memory_space=pltpu.SMEM)
    vmem = pl.BlockSpec(memory_space=pltpu.VMEM)
    anys = pl.BlockSpec(memory_space=pl.ANY)
    atm, ocean, flux = pl.pallas_call(
        kernel,
        out_shape=(
            jax.ShapeDtypeStruct((ROWS, LEV, LON), BF16),
            jax.ShapeDtypeStruct((OLEV, OX, 128), F32),
            jax.ShapeDtypeStruct((OX, 128), F32),
        ),
        in_specs=[smem, smem, anys, anys, vmem, vmem, vmem, vmem, vmem, anys]
        + [vmem] * 7,
        out_specs=(vmem, vmem, vmem),
        scratch_shapes=[
            pltpu.VMEM((ROWS, LEV, LON), BF16),
            pltpu.VMEM((LON, LON), BF16),
            pltpu.VMEM((384, LON), BF16),
            pltpu.VMEM((10, NW, 128), F32),
            pltpu.VMEM((ND * MSG, 128), F32),
            pltpu.VMEM((ND, MSG, 128), BF16),
            pltpu.VMEM((ND, MSG, 128), BF16),
            pltpu.VMEM((ND, MSG, 128), BF16),
            pltpu.VMEM((SLOTS, WAVES, WAVES), BF16),
            pltpu.VMEM((COLS * WAVES, 128), F32),
            pltpu.VMEM((COLS * WAVES, 128), F32),
            pltpu.VMEM((LON, 384), BF16),
            pltpu.VMEM((160, 128), BF16),
            pltpu.VMEM((PAIRS, 128, 128), BF16),
            pltpu.VMEM((NW, 8, 128), F32),
            pltpu.VMEM((NW, 8, 128), F32),
            pltpu.VMEM((FIELDS, OX, 128), F32),
            pltpu.VMEM((2, FIELDS, HALO, 128), F32),
            pltpu.VMEM((2, FIELDS, HALO, 128), F32),
            pltpu.VMEM((2, OX, 128), F32),
            pltpu.VMEM((2, EXT, 128), F32),
            pltpu.VMEM((FIELDS, EXT, 256), F32),
            pltpu.SemaphoreType.REGULAR((2,)),
            pltpu.SemaphoreType.DMA((3,)),
            pltpu.SemaphoreType.DMA(()),
            pltpu.SemaphoreType.DMA(()),
            pltpu.SemaphoreType.DMA(()),
            pltpu.SemaphoreType.DMA(()),
            pltpu.SemaphoreType.DMA(()),
            pltpu.SemaphoreType.DMA(()),
            pltpu.SemaphoreType.DMA((8,)),
            pltpu.SemaphoreType.DMA((8,)),
        ],
        compiler_params=pltpu.CompilerParams(
            collective_id=0, has_side_effects=True, vmem_limit_bytes=60 * 1024 * 1024
        ),
        name="step",
    )(
        wave_of_slot,
        lat_of_row,
        grid_field.transpose(1, 0, 2),
        legendre,
        wave_of_slot,
        analysis,
        synthesis,
        mode_rates.reshape(1, NLEV),
        flux_weights.reshape(1, NLEV),
        remap_mats,
        pair_dest.reshape(NW // 2, 128),
        pair_src.reshape(NW // 2, 128),
        pair_dst.reshape(NW // 2, 128),
        ocean_temp,
        diffusivity,
        surface_heat,
        land_mask,
    )
    atm, ocean, flux = pl.pallas_call(
        hand_over,
        out_shape=tuple(jax.ShapeDtypeStruct(v.shape, v.dtype) for v in (atm, ocean, flux)),
        in_specs=[anys] * 3,
        out_specs=(anys,) * 3,
        scratch_shapes=[
            pltpu.VMEM((ROWS, LEV, LON), BF16),
            pltpu.VMEM((OLEV, OX, 128), F32),
            pltpu.VMEM((OX, 128), F32),
            pltpu.SemaphoreType.DMA((ROWS + 2,)),
            pltpu.SemaphoreType.DMA((ROWS + 2,)),
        ],
        name="hand_over",
    )(atm, ocean, flux)
    return atm.transpose(1, 0, 2), ocean, flux


def solution(mesh):
    return jax.shard_map(
        per_device,
        mesh=mesh,
        in_specs=(
            P("lev", "wav", None),
            P("wav", None, None),
            P(),
            P("wav"),
            P(),
            P(),
            P(),
            P(),
            P("lev", "wav", None, None),
            P("lev", None, None),
            P("lev", None),
            P("lev", None),
            P(None, "lev", "wav"),
            P("lev", "wav"),
            P("lev", "wav"),
            P("lev", "wav"),
        ),
        out_specs=(P("lev", "wav", None), P(None, "lev", "wav"), P("lev", "wav")),
        check_vma=False,
    )
```

```python
import functools
import math

import jax
import jax.numpy as jnp
from jax import lax
from jax.experimental import pallas as pl
from jax.experimental.pallas import tpu as pltpu
from jax.sharding import PartitionSpec as P

MESH = pl.DeviceIdType.MESH
F32 = jnp.float32
BF16 = jnp.bfloat16
HIGH = lax.Precision.HIGHEST

SWEEPS = 4
NG = 4
NW = 64
ND = NG * NW
LEV = 32
ROWS = 10
LON = 1280
WAVES = 640
NLEV = 128
COLS = 5
SLOTS = 3
MSG = 16
SENT = 14
PAIRS = 64
OX = 48
OLEV = 8
HALO = 8
EXT = OX + 2 * HALO
FIELDS = OLEV + 3

SIN_POLY = (6.28318528, -41.34168068, 81.60248108, -76.58128818, 39.76072297)


def nt(a, b):
    return lax.dot_general(a, b, (((1,), (1,)), ((), ())), preferred_element_type=F32)


def tn(a, b, precision=None):
    return lax.dot_general(
        a, b, (((0,), (0,)), ((), ())), preferred_element_type=F32, precision=precision
    )


def cos_turns(phase, scale):
    whole = jnp.floor(phase * (1.0 / LON) + 0.5)
    rest = jnp.abs(phase - whole * LON)
    t = (LON / 4 - rest) * (1.0 / LON)
    z = t * t
    c = [scale * v for v in SIN_POLY]
    return t * (c[0] + z * (c[1] + z * (c[2] + z * (c[3] + z * c[4]))))


def swap_blocks(v, lane):
    low = lane < 64
    even = lax.rem(lane // 32, 2) == 0
    a0 = jnp.where(low, v[0], pltpu.roll(v[2], 64, 1))
    a2 = jnp.where(low, pltpu.roll(v[0], 64, 1), v[2])
    a1 = jnp.where(low, v[1], pltpu.roll(v[3], 64, 1))
    a3 = jnp.where(low, pltpu.roll(v[1], 64, 1), v[3])
    return (
        jnp.where(even, a0, pltpu.roll(a1, 32, 1)),
        jnp.where(even, pltpu.roll(a0, 96, 1), a1),
        jnp.where(even, a2, pltpu.roll(a3, 32, 1)),
        jnp.where(even, pltpu.roll(a2, 96, 1), a3),
    )


def lanes(shape):
    return lax.broadcasted_iota(jnp.int32, shape, len(shape) - 1)


def down(row):
    return jnp.broadcast_to(row, (128, 128)).T


def kernel(
    wos_s,
    lat_s,
    field_in,
    legendre,
    wos_v,
    analysis,
    synthesis,
    rates,
    weights,
    mats,
    p_dest,
    p_src,
    p_dst,
    temp,
    kappa,
    heat,
    mask,
    atm,
    ocean,
    flux,
    field,
    table,
    rows_in,
    waves,
    acc,
    out1,
    in1,
    in2,
    leg,
    cols_f,
    flux_f,
    lhs,
    segs,
    mats_v,
    out3,
    in3,
    edge,
    rows_edge,
    in_rows,
    slab,
    in_slab,
    ext,
    ready,
    local_sem,
    send1,
    recv1,
    send2,
    recv2,
    send3,
    recv3,
    send4,
    recv4,
):
    g = lax.axis_index("lev")
    w = lax.axis_index("wav")
    me = g * NW + w
    barrier = pltpu.get_barrier_semaphore()
    out3_rows = out3.reshape(NW * 8, 128)
    in3_rows = in3.reshape(NW * 8, 128)

    field_copy = pltpu.make_async_copy(field_in, field, local_sem.at[2])
    field_copy.start()
    first_slot = (COLS * g) // 2
    leg_copy = pltpu.make_async_copy(
        legendre.at[pl.ds(first_slot, SLOTS)], leg, local_sem.at[0]
    )
    leg_copy.start()
    mats_copy = pltpu.make_async_copy(mats.at[0], mats_v, local_sem.at[1])
    mats_copy.start()

    outer, inner = w // 8, lax.rem(w, 8)
    far = [(g, lax.rem(outer + j, 8) * 8 + inner) for j in range(1, 8)]
    near = [(g, outer * 8 + lax.rem(inner + j, 8)) for j in range(1, 8)]
    across = [(lax.rem(g + j, NG), w) for j in range(1, NG)]

    def tell(sem, partners):
        for partner in partners:
            pl.semaphore_signal(sem, inc=1, device_id=partner, device_id_type=MESH)

    tell(barrier, far + near + across)
    field_copy.wait()

    for r in range(ROWS):
        rows_in[r * LEV : (r + 1) * LEV, :] = field[r]
    rows_in[320:352, :] = field[8]
    rows_in[352:384, :] = field[9]

    sub_w = lax.broadcasted_iota(jnp.int32, (NW, WAVES), 0)
    at_slot = lanes((NW, WAVES)) - 10 * sub_w
    all_waves = jnp.broadcast_to(wos_v[...].reshape(1, WAVES).astype(F32), (NW, WAVES))
    for k in range(10):
        m = jnp.sum(jnp.where(at_slot == k, all_waves, 0.0), axis=1, keepdims=True)
        waves[k] = jnp.broadcast_to(m, (NW, 128))

    ocean_mask = mask[...].astype(F32)
    for k in range(OLEV):
        edge[k] = temp[k] * ocean_mask
    edge[OLEV] = ocean_mask
    edge[OLEV + 1] = kappa[...]
    edge[OLEV + 2] = heat[...]
    lane48 = lanes((OX, 128))
    left = jnp.zeros((OX, 128), F32)
    right = jnp.zeros((OX, 128), F32)
    for k in range(FIELDS):
        here = lane48 // 4 == k
        v = edge[k]
        left = jnp.where(here, pltpu.roll(v, 4 * k, 1) if k else v, left)
        right = jnp.where(here, pltpu.roll(v, (4 * k + 4) % 128, 1), right)
        rows_edge[0, k] = v[:HALO]
        rows_edge[1, k] = v[OX - HALO :]
    slab[0] = left
    slab[1] = right

    up, dn = lax.rem(g + NG - 1, NG), lax.rem(g + 1, NG)
    wl, wr = lax.rem(w + NW - 1, NW), lax.rem(w + 1, NW)

    def ocean_copies():
        c = []
        c.append((rows_edge.at[0], in_rows.at[1], (up, w)))
        c.append((rows_edge.at[1], in_rows.at[0], (dn, w)))
        for side, ww in ((0, wl), (1, wr)):
            c.append((slab.at[side], in_slab.at[1 - side, pl.ds(HALO, OX)], (g, ww)))
            c.append(
                (slab.at[side, pl.ds(0, HALO)], in_slab.at[1 - side, pl.ds(HALO + OX, HALO)], (up, ww))
            )
            c.append(
                (slab.at[side, pl.ds(OX - HALO, HALO)], in_slab.at[1 - side, pl.ds(0, HALO)], (dn, ww))
            )
        return [
            pltpu.make_async_remote_copy(
                src_ref=s, dst_ref=d, send_sem=send4.at[i], recv_sem=recv4.at[i],
                device_id=dev, device_id_type=MESH,
            )
            for i, (s, d, dev) in enumerate(c)
        ]

    lane64 = lanes((NW, 128))
    pl.semaphore_wait(barrier, len(far) + len(near) + len(across))
    tell(ready.at[0], near)

    def make_group(i, c):
        gg = lax.rem(g + i, NG)
        base = pl.multiple_of(gg * (COLS * NW), NW)
        for cl in range(COLS):
            q = gg * COLS + cl
            m = waves[q // 2]
            shift = (lax.rem(q, 2) * (LON // 4)).astype(F32)
            scale = math.sqrt(2.0 / LON)
            phase = m * lane64.astype(F32) + shift
            now = cos_turns(phase, scale)
            before = cos_turns(phase - 128.0 * m, scale)
            twice = cos_turns(128.0 * m, 2.0)
            for a in range(10):
                table[pl.ds(base + cl * NW, NW), a * 128 : (a + 1) * 128] = now.astype(BF16)
                now, before = twice * now - before, now
        @pl.when(i == 0)
        def _():
            pl.semaphore_wait(ready.at[0], len(near))
            tell(ready.at[1], across)

        out = nt(table[pl.ds(base, COLS * NW), :], rows_in[...])
        start = pl.multiple_of(gg * (NW * MSG), NW * MSG)
        prev = None
        for cl in range(COLS):
            o = out[cl * NW : (cl + 1) * NW]
            acc[pl.ds(start + 2 * cl, NW, stride=MSG), :] = o[:, :128]
            acc[pl.ds(start + 2 * cl + 1, NW, stride=MSG), :] = o[:, 128:256]
            if cl % 2 == 0:
                prev = o[:, 256:384]
            if cl % 2 == 1 or cl == COLS - 1:
                acc[pl.ds(start + 10 + cl // 2, NW, stride=MSG), :] = jnp.where(
                    lane64 < 64, prev, o[:, 256:384]
                )
        out1[pl.ds(gg * NW, NW)] = (
            acc[pl.ds(start, NW * MSG), :].reshape(NW, MSG, 128).astype(BF16)
        )

        @pl.when(i == 0)
        def _():
            pl.semaphore_wait(ready.at[1], len(across))
            for copy in ocean_copies():
                copy.start()
            in1[me] = out1[me]

        def send(j, c):
            there = lax.rem(w + j, NW)
            pltpu.make_async_remote_copy(
                src_ref=out1.at[gg * NW + there, pl.ds(0, SENT)],
                dst_ref=in1.at[me, pl.ds(0, SENT)],
                send_sem=send1,
                recv_sem=recv1,
                device_id=(gg, there),
                device_id_type=MESH,
            ).start()
            return c

        lax.fori_loop(jnp.where(i == 0, 1, 0), NW, send, 0)
        return c

    lax.fori_loop(0, NG, make_group, 0)

    for copy in ocean_copies():
        copy.wait()
    sub_e = lax.broadcasted_iota(jnp.int32, (EXT, 256), 0)
    lane_e = lanes((EXT, 256))
    inside_rows = jnp.logical_and(
        jnp.logical_or(sub_e >= HALO, g > 0),
        jnp.logical_or(sub_e < HALO + OX, g < NG - 1),
    )
    inside = jnp.logical_and(
        inside_rows,
        jnp.logical_and(
            jnp.logical_or(lane_e < 252, w > 0),
            jnp.logical_or(jnp.logical_or(lane_e < 128, lane_e >= 252), w < NW - 1),
        ),
    )
    lane_m = lanes((EXT, 128))
    for k in range(FIELDS):
        ext[k, :HALO, :128] = in_rows[0, k]
        ext[k, HALO : HALO + OX, :128] = edge[k]
        ext[k, HALO + OX :, :128] = in_rows[1, k]
        from_left = pltpu.roll(in_slab[0], (124 - 4 * k) % 128, 1)
        from_right = pltpu.roll(in_slab[1], (128 - 4 * k) % 128, 1) if k else in_slab[1]
        ext[k, :, 128:] = jnp.where(
            lane_m >= 124, from_left, jnp.where(lane_m < 4, from_right, 0.0)
        )
    e_mask = jnp.where(inside, ext[OLEV], 0.0)
    ext[OLEV] = e_mask
    for k in range(2):
        ext[OLEV + 1 + k] = jnp.where(inside, ext[OLEV + 1 + k], 0.0)

    def level(k, c):
        cur = jnp.where(inside, ext[k], 0.0)
        add = jnp.where(k == 0, 1.0, 0.0).astype(F32) * ext[OLEV + 2]
        for _ in range(SWEEPS):
            lap = (
                pltpu.roll(cur, EXT - 1, 0)
                + pltpu.roll(cur, 1, 0)
                + pltpu.roll(cur, 255, 1)
                + pltpu.roll(cur, 1, 1)
                - 4.0 * cur
            )
            cur = ext[OLEV] * (cur + ext[OLEV + 1] * lap + add)
        ocean[k] = cur[HALO : HALO + OX, :128]
        return c

    lax.fori_loop(0, OLEV, level, 0)

    sub_p = lax.broadcasted_iota(jnp.int32, (128, 128), 0)
    lane_p = lanes((128, 128))
    upper = jnp.logical_and(sub_p < lane_p, sub_p // PAIRS == lane_p // PAIRS).astype(BF16)
    hits = p_dest[...] == w
    rank_in = jnp.dot(hits.astype(BF16), upper, preferred_element_type=F32)
    lane_h = lanes((NW // 2, 128))
    dst_in = p_dst[...].astype(F32) + 1.0
    pick_in = {}
    for half in range(2):
        mine = jnp.logical_and(hits, lane_h // PAIRS == half)
        for s in range(2):
            chosen_s = jnp.logical_and(mine, rank_in == float(s))
            row_of = jnp.sum(jnp.where(chosen_s, dst_in, 0.0), axis=1, keepdims=True)
            pick_in[half, s] = (lane_h.astype(F32) + 1.0 == row_of).astype(F32)

    def my_row(ref):
        row = ref[pl.ds(w // 2, 1), :]
        return jnp.where(lax.rem(w, 2) == 1, pltpu.roll(row, PAIRS, 1), row)[:, :PAIRS]

    my_dest = my_row(p_dest)
    my_src = my_row(p_src)
    same = lax.broadcasted_iota(jnp.int32, (NW, PAIRS), 0) == my_dest
    counts = jnp.dot(
        same.astype(BF16), upper[:PAIRS, :PAIRS], preferred_element_type=F32
    )
    rank_out = jnp.sum(jnp.where(same, counts, 0.0), axis=0, keepdims=True)
    pick_out = [
        jnp.logical_and(same, rank_out == float(s)).astype(F32) for s in range(2)
    ]
    src_row = my_src // 10
    seg_at = (my_src - src_row * 10) * 16 + src_row
    pick_seg = (lax.broadcasted_iota(jnp.int32, (160, PAIRS), 0) == seg_at).astype(BF16)

    degree = lanes((NLEV, WAVES))
    base = (degree * (degree + 1)).astype(F32) / float(WAVES * WAVES)
    rate = down(rates[...])
    weight = down(weights[...])
    damping = 1.0 / (1.0 + jnp.concatenate([rate] * 5, axis=1) * base)
    leg_copy.wait()

    def all_but_one(send_sem, recv_sem, src, dst):
        return pltpu.make_async_remote_copy(
            src_ref=src.at[pl.ds(0, ND - 1), pl.ds(0, SENT)],
            dst_ref=dst.at[pl.ds(0, ND - 1), pl.ds(0, SENT)],
            send_sem=send_sem,
            recv_sem=recv_sem,
            device_id=(g, w),
            device_id_type=MESH,
        )

    def widen(src):
        def step(i, c):
            n = ND // 16
            acc[pl.ds(pl.multiple_of(i * n * MSG, n * MSG), n * MSG), :] = (
                src[pl.ds(i * n, n)].astype(F32).reshape(n * MSG, 128)
            )
            return c

        lax.fori_loop(0, 16, step, 0)

    first = all_but_one(send1, recv1, out1, in1)
    first.wait_send()
    first.wait_recv()
    widen(in1)

    def at(ref, start, n, stride):
        return ref[pl.ds(start, n, stride=stride), :]

    for cl in range(COLS):
        for t in range(2):
            v = [at(acc, k * NW * MSG + 2 * cl + t, NW, MSG) for k in range(NG)]
            for q, out in enumerate(swap_blocks(v, lane64)):
                cols_f[pl.ds(cl * WAVES + 4 * t + q, NW, stride=ROWS), :] = out
    for p in range(3):
        v = [at(acc, k * NW * MSG + 10 + p, NW, MSG) for k in range(NG)]
        for q, out in enumerate(swap_blocks(v, lane64)):
            if 2 * p + q // 2 < COLS:
                cols_f[pl.ds((2 * p + q // 2) * WAVES + 8 + q % 2, NW, stride=ROWS), :] = out

    odd = lax.rem(g, 2)

    for cl in range(COLS):
        here = pl.ds(cl * WAVES, WAVES)
        table_of = leg[(odd + cl) // 2]
        m = wos_s[w * 10 + (COLS * g + cl) // 2]
        spectra = jnp.dot(
            cols_f[here, :].T.astype(BF16), table_of, preferred_element_type=F32
        )
        spectra = jnp.where(degree >= m, spectra, 0.0).astype(BF16)
        modal = jnp.dot(analysis[...], spectra, preferred_element_type=F32)
        modal = (modal * damping).astype(BF16)
        solved = jnp.dot(synthesis[...], modal, preferred_element_type=F32).astype(BF16)
        flux_coef = jnp.concatenate(
            [
                jnp.sum(
                    weight * solved[:, b * 128 : (b + 1) * 128].astype(F32),
                    axis=0,
                    keepdims=True,
                )
                for b in range(5)
            ],
            axis=1,
        )
        right = jnp.concatenate(
            [solved, jnp.broadcast_to(flux_coef, (128, WAVES)).astype(BF16)], axis=0
        )
        back = nt(table_of, right)
        cols_f[here, :] = back[:, :128]
        flux_f[here, :] = back[:, 128:]

    for cl in range(COLS):
        for t in range(2):
            v = [at(cols_f, cl * WAVES + 4 * t + q, NW, ROWS) for q in range(NG)]
            for k, out in enumerate(swap_blocks(v, lane64)):
                acc[pl.ds(k * NW * MSG + 2 * cl + t, NW, stride=MSG), :] = out
    fluxes = jnp.zeros((NW, 128), F32)
    for cl in range(COLS):
        for r in range(ROWS):
            fluxes = jnp.where(
                lane64 == 64 + cl * ROWS + r, at(flux_f, cl * WAVES + r, NW, ROWS), fluxes
            )
    for p in range(3):
        v = []
        for q in range(4):
            cl = min(2 * p + q // 2, COLS - 1)
            v.append(at(cols_f, cl * WAVES + 8 + q % 2, NW, ROWS))
        for k, out in enumerate(swap_blocks(v, lane64)):
            if p == 2:
                out = jnp.where(lane64 < 64, out, fluxes)
            acc[pl.ds(k * NW * MSG + 10 + p, NW, stride=MSG), :] = out

    def send_group(i, c):
        gg = lax.rem(g + i, NG)
        start = pl.multiple_of(gg * (NW * MSG), NW * MSG)
        out1[pl.ds(gg * NW, NW)] = (
            acc[pl.ds(start, NW * MSG), :].reshape(NW, MSG, 128).astype(BF16)
        )

        @pl.when(i == 0)
        def _():
            in2[me] = out1[me]

        def send(j, c):
            there = lax.rem(w + j, NW)
            pltpu.make_async_remote_copy(
                src_ref=out1.at[gg * NW + there, pl.ds(0, SENT)],
                dst_ref=in2.at[me, pl.ds(0, SENT)],
                send_sem=send2,
                recv_sem=recv2,
                device_id=(gg, there),
                device_id_type=MESH,
            ).start()
            return c

        lax.fori_loop(jnp.where(i == 0, 1, 0), NW, send, 0)
        return c

    lax.fori_loop(0, NG, send_group, 0)
    mats_copy.wait()
    second = all_but_one(send2, recv2, out1, in2)
    second.wait_send()
    second.wait_recv()
    widen(in2)

    for k in range(NG):
        f12 = at(acc, k * NW * MSG + 12, NW, MSG)
        for cl in range(COLS):
            rows = pl.ds((k * COLS + cl) * NW, NW)
            v = at(acc, k * NW * MSG + 10 + cl // 2, NW, MSG) if cl < 4 else f12
            if cl % 2 == 1:
                v = pltpu.roll(v, 64, 1)
            f = pltpu.roll(f12, 128 - cl * ROWS, 1) if cl else f12
            lhs[rows, 256:384] = jnp.where(
                lane64 < 64, v, jnp.where(lane64 < 64 + ROWS, f, 0.0)
            ).astype(BF16)
    last = tn(lhs[:, 256:384], table[...])
    mu = [
        -cos_turns(jnp.full((LEV, 128), lat_s[r], jnp.int32).astype(F32) + 0.5, 1.0)
        for r in range(ROWS)
    ]

    def finish(r, grid):
        for jt in range(10):
            cut = slice(jt * 128, (jt + 1) * 128)
            atm[r, :, cut] = (
                grid[:, cut] * (1.0 + field[r, :, cut].astype(F32) * mu[r])
            ).astype(BF16)

    for jt in range(10):
        segs[jt * 16 : (jt + 1) * 16, :] = last[64:80, jt * 128 : (jt + 1) * 128].astype(BF16)
    chosen = tn(pick_seg, segs[...]).astype(BF16)
    sub8 = lax.broadcasted_iota(jnp.int32, (8, 128), 0)
    parts = []
    for b in range(PAIRS // 8):
        total = jnp.zeros((8, 128), F32)
        eight = chosen[b * 8 : (b + 1) * 8]
        for u in range(8):
            total = jnp.where(sub8 == u, nt(eight, mats_v[b * 8 + u]), total)
        parts.append(total)
    products = jnp.concatenate(parts, axis=0)
    for s in range(2):
        out3_rows[pl.ds(s, NW, stride=8), :] = jnp.dot(
            pick_out[s], products, precision=HIGH, preferred_element_type=F32
        )
    in3[w] = out3[w]

    def send_flux(j, c):
        there = lax.rem(w + j, NW)
        pltpu.make_async_remote_copy(
            src_ref=out3.at[there, pl.ds(0, 2)],
            dst_ref=in3.at[w, pl.ds(0, 2)],
            send_sem=send3,
            recv_sem=recv3,
            device_id=(g, there),
            device_id_type=MESH,
        ).start()
        return c

    lax.fori_loop(1, NW, send_flux, 0)

    for r in range(2):
        finish(8 + r, last[r * LEV : (r + 1) * LEV])
    for k in range(NG):
        for cl in range(COLS):
            for t in range(2):
                lhs[pl.ds((k * COLS + cl) * NW, NW), t * 128 : (t + 1) * 128] = at(
                    acc, k * NW * MSG + 2 * cl + t, NW, MSG
                ).astype(BF16)
    for t in range(2):
        main = tn(lhs[:, t * 128 : (t + 1) * 128], table[...])
        for q in range(4):
            finish(4 * t + q, main[q * LEV : (q + 1) * LEV])

    third = pltpu.make_async_remote_copy(
        src_ref=out3.at[pl.ds(0, NW - 1), pl.ds(0, 2)],
        dst_ref=in3.at[pl.ds(0, NW - 1), pl.ds(0, 2)],
        send_sem=send3,
        recv_sem=recv3,
        device_id=(g, w),
        device_id_type=MESH,
    )
    third.wait_send()
    third.wait_recv()
    summed = jnp.zeros((128, 128), F32)
    for half in range(2):
        for s in range(2):
            summed = summed + tn(
                pick_in[half, s], at(in3_rows, half * 8 + s, NW // 2, 16), HIGH
            )
    flux[...] = summed[:OX]


def hand_over(atm_in, ocean_in, flux_in, atm, ocean, flux, atm_v, ocean_v, flux_v, came, went):
    parts = [(atm_in.at[r], atm_v.at[r], atm.at[r]) for r in range(ROWS)]
    parts += [(ocean_in, ocean_v, ocean), (flux_in, flux_v, flux)]
    ins = [pltpu.make_async_copy(a, v, came.at[i]) for i, (a, v, _) in enumerate(parts)]
    outs = [pltpu.make_async_copy(v, b, went.at[i]) for i, (_, v, b) in enumerate(parts)]
    for copy in ins:
        copy.start()
    for come, go in zip(ins, outs):
        come.wait()
        go.start()
    for copy in outs:
        copy.wait()


def per_device(
    grid_field,
    legendre,
    wave_of_slot,
    lat_of_row,
    analysis,
    synthesis,
    mode_rates,
    flux_weights,
    remap_mats,
    pair_dest,
    pair_src,
    pair_dst,
    ocean_temp,
    diffusivity,
    surface_heat,
    land_mask,
):
    smem = pl.BlockSpec(memory_space=pltpu.SMEM)
    vmem = pl.BlockSpec(memory_space=pltpu.VMEM)
    anys = pl.BlockSpec(memory_space=pl.ANY)
    atm, ocean, flux = pl.pallas_call(
        kernel,
        out_shape=(
            jax.ShapeDtypeStruct((ROWS, LEV, LON), BF16),
            jax.ShapeDtypeStruct((OLEV, OX, 128), F32),
            jax.ShapeDtypeStruct((OX, 128), F32),
        ),
        in_specs=[smem, smem, anys, anys, vmem, vmem, vmem, vmem, vmem, anys]
        + [vmem] * 7,
        out_specs=(vmem, vmem, vmem),
        scratch_shapes=[
            pltpu.VMEM((ROWS, LEV, LON), BF16),
            pltpu.VMEM((LON, LON), BF16),
            pltpu.VMEM((384, LON), BF16),
            pltpu.VMEM((10, NW, 128), F32),
            pltpu.VMEM((ND * MSG, 128), F32),
            pltpu.VMEM((ND, MSG, 128), BF16),
            pltpu.VMEM((ND, MSG, 128), BF16),
            pltpu.VMEM((ND, MSG, 128), BF16),
            pltpu.VMEM((SLOTS, WAVES, WAVES), BF16),
            pltpu.VMEM((COLS * WAVES, 128), F32),
            pltpu.VMEM((COLS * WAVES, 128), F32),
            pltpu.VMEM((LON, 384), BF16),
            pltpu.VMEM((160, 128), BF16),
            pltpu.VMEM((PAIRS, 128, 128), BF16),
            pltpu.VMEM((NW, 8, 128), F32),
            pltpu.VMEM((NW, 8, 128), F32),
            pltpu.VMEM((FIELDS, OX, 128), F32),
            pltpu.VMEM((2, FIELDS, HALO, 128), F32),
            pltpu.VMEM((2, FIELDS, HALO, 128), F32),
            pltpu.VMEM((2, OX, 128), F32),
            pltpu.VMEM((2, EXT, 128), F32),
            pltpu.VMEM((FIELDS, EXT, 256), F32),
            pltpu.SemaphoreType.REGULAR((2,)),
            pltpu.SemaphoreType.DMA((3,)),
            pltpu.SemaphoreType.DMA(()),
            pltpu.SemaphoreType.DMA(()),
            pltpu.SemaphoreType.DMA(()),
            pltpu.SemaphoreType.DMA(()),
            pltpu.SemaphoreType.DMA(()),
            pltpu.SemaphoreType.DMA(()),
            pltpu.SemaphoreType.DMA((8,)),
            pltpu.SemaphoreType.DMA((8,)),
        ],
        compiler_params=pltpu.CompilerParams(
            collective_id=0, has_side_effects=True, vmem_limit_bytes=60 * 1024 * 1024
        ),
        name="step",
    )(
        wave_of_slot,
        lat_of_row,
        grid_field.transpose(1, 0, 2),
        legendre,
        wave_of_slot,
        analysis,
        synthesis,
        mode_rates.reshape(1, NLEV),
        flux_weights.reshape(1, NLEV),
        remap_mats,
        pair_dest.reshape(NW // 2, 128),
        pair_src.reshape(NW // 2, 128),
        pair_dst.reshape(NW // 2, 128),
        ocean_temp,
        diffusivity,
        surface_heat,
        land_mask,
    )
    atm, ocean, flux = pl.pallas_call(
        hand_over,
        out_shape=tuple(jax.ShapeDtypeStruct(v.shape, v.dtype) for v in (atm, ocean, flux)),
        in_specs=[anys] * 3,
        out_specs=(anys,) * 3,
        scratch_shapes=[
            pltpu.VMEM((ROWS, LEV, LON), BF16),
            pltpu.VMEM((OLEV, OX, 128), F32),
            pltpu.VMEM((OX, 128), F32),
            pltpu.SemaphoreType.DMA((ROWS + 2,)),
            pltpu.SemaphoreType.DMA((ROWS + 2,)),
        ],
        name="hand_over",
    )(atm, ocean, flux)
    return atm.transpose(1, 0, 2), ocean, flux


def solution(mesh):
    return jax.shard_map(
        per_device,
        mesh=mesh,
        in_specs=(
            P("lev", "wav", None),
            P("wav", None, None),
            P(),
            P("wav"),
            P(),
            P(),
            P(),
            P(),
            P("lev", "wav", None, None),
            P("lev", None, None),
            P("lev", None),
            P("lev", None),
            P(None, "lev", "wav"),
            P("lev", "wav"),
            P("lev", "wav"),
            P("lev", "wav"),
        ),
        out_specs=(P("lev", "wav", None), P(None, "lev", "wav"), P("lev", "wav")),
        check_vma=False,
    )
```
